256 devices in a mesh: row: 32 (over x, z), col: 8 (over y, core).
Axes of the slice: x: 4, y: 4, z: 8, core: 2. Of those that a mesh axis runs over, the one named last changes fastest.
Arguments:
- panel_block: float32 [16384, 128], P('row'), may hold values from -8 to 8, as said below
- trailing: float32 [16384, 16384], P('row', 'col'), may hold values from -80 to 80
Outputs:
- reduced: float32 [16384, 16384], P('row', 'col')
- band_block: float32 [128, 128], replicated
- first_factor: float32 [128, 128], replicated
The draws below stay inside these ranges and needn't reach their ends.
Inputs may be any that keep to these rules, and one draw needn't show every extreme that they name: `panel_block`: entries of order the inverse square root of 16384; rows may differ in scale; the columns may be nearly dependent, with a condition number of the panel up to a few thousand; the first 128 rows of the orthonormal basis have spectral norm at most 0.8, so that I + top^T needs no pivoting.
All inputs are finite; a program needn't handle non-finite values.
Results may differ from the reference program's by a relative error of at most 0.0017.
Values sent between devices are 32-bit elements; how exact they have to be, the bound alone decides.
A program may use at most 128 MiB of HBM per device.

```python
import math
import jax
import jax.numpy as jnp
from jax import lax

N = 16384
B = 128


def draw_panel_block(key, part):
    first_key = jax.random.fold_in(jax.random.fold_in(key, 11), 0)
    second_key = jax.random.fold_in(jax.random.fold_in(key, 11), 1)
    fourth_key = jax.random.fold_in(jax.random.fold_in(key, 11), 3)
    common = jnp.clip(jax.random.normal(first_key, (N, 1), jnp.float32), -6.0, 6.0)
    own_part = jnp.clip(jax.random.normal(second_key, (N, B), jnp.float32), -6.0, 6.0)
    half_width = B // 2
    steps_down = jnp.minimum(jnp.arange(B, dtype=jnp.float32), float(half_width - 1))
    grade = jnp.exp(steps_down * (math.log(0.006) / (half_width - 1)))
    order = jax.random.permutation(fourth_key, B)
    grade = grade[order]
    values = (common + own_part * grade[None, :]) / jnp.sqrt(1.0 + grade * grade)[None, :]
    rising = jnp.exp(jnp.arange(N, dtype=jnp.float32) * (math.log(3.0) / N))[:, None]
    leading = jnp.where(jnp.arange(N) < B, 12.0, 1.0).astype(jnp.float32)[:, None]
    values = values * rising * leading
    return jnp.clip(values * float(N) ** (-0.5), -8.0, 8.0)


def draw_trailing(key, part):
    first_key = jax.random.fold_in(jax.random.fold_in(key, 23), 0)
    base = jnp.clip(jax.random.normal(first_key, (N, N), jnp.float32), -6.0, 6.0)
    values = (base + base.T) * 0.7071
    return jnp.clip(values, -80.0, 80.0)


def setup_inputs(seed: int = 0) -> dict:
    streams_of = jax.random.split(jax.random.key(seed), 3)
    panel_block = draw_panel_block(jax.random.fold_in(streams_of[2], 71), 0)
    trailing = draw_trailing(jax.random.fold_in(streams_of[2], 71), 0)
    return {"panel_block": panel_block, "trailing": trailing}


HIGH = lax.Precision.HIGHEST

def gram_of(values):
    return jnp.dot(values.T, values, precision=HIGH, preferred_element_type=values.dtype)

def invert_square(square):
    size_n = square.shape[0]
    augmented = jnp.concatenate([square, jnp.eye(size_n, dtype=square.dtype)], axis=1)
    positions = jnp.arange(size_n)

    def eliminate(pivot, current):
        pivot_row = lax.dynamic_index_in_dim(current, pivot, 0, keepdims=False)
        pivot_row = pivot_row / pivot_row[pivot]
        column = lax.dynamic_index_in_dim(current, pivot, 1, keepdims=False)
        column = column - (positions == pivot).astype(current.dtype)
        return current - column[:, None] * pivot_row[None, :]
    augmented = lax.fori_loop(0, size_n, eliminate, augmented)
    return augmented[:, size_n:]

def right_solve(factor, values):
    return lax.linalg.triangular_solve(factor, values, left_side=False, lower=True, transpose_a=True)

def reference(panel_block, trailing):
    first_factor = jnp.linalg.cholesky(gram_of(panel_block))
    first_basis = right_solve(first_factor, panel_block)
    second_factor = jnp.linalg.cholesky(gram_of(first_basis))
    basis = right_solve(second_factor, first_basis)
    band_block = -jnp.dot(second_factor.T, first_factor.T, precision=HIGH)
    width = basis.shape[1]
    kernel = invert_square(jnp.eye(width, dtype=basis.dtype) + basis[:width].T)
    ident = (jnp.arange(basis.shape[0])[:, None] == jnp.arange(width)[None, :]).astype(basis.dtype)
    vectors = basis + ident
    applied = jnp.dot(jnp.dot(trailing, vectors, precision=HIGH), kernel, precision=HIGH)
    inner = jnp.dot(kernel.T, jnp.dot(vectors.T, applied, precision=HIGH), precision=HIGH)
    update = applied - 0.5 * jnp.dot(vectors, inner, precision=HIGH)
    reduced = trailing - jnp.dot(vectors, update.T, precision=HIGH) - jnp.dot(update, vectors.T, precision=HIGH)
    return (reduced, band_block, first_factor)
```

```python
import functools

import jax
import jax.numpy as jnp
from jax import lax
from jax.experimental import pallas as pl
from jax.experimental.pallas import tpu as pltpu
from jax.sharding import PartitionSpec as P

HIGH = lax.Precision.HIGHEST
F32 = jnp.float32
BF16 = jnp.bfloat16
MESH = pl.DeviceIdType.MESH
NX, NZ = 4, 8
NN = (((1,), (0,)), ((), ()))
NT = (((1,), (1,)), ((), ()))
TN = (((0,), (0,)), ((), ()))


def mm(a, b, dims=NN):
    return lax.dot_general(a, b, dims, precision=HIGH, preferred_element_type=F32)


def halves(a):
    top = a.astype(BF16)
    return top, (a - top.astype(F32)).astype(BF16)


def mm3(a, b, dims=NN):
    def one(p, q):
        return lax.dot_general(p, q, dims, preferred_element_type=F32)
    return one(a[0], b[0]) + (one(a[0], b[1]) + one(a[1], b[0]))


def eyes(shape, shift=0):
    return (lax.broadcasted_iota(jnp.int32, shape, 0) + shift) == lax.broadcasted_iota(jnp.int32, shape, 1)


def chol_inv(work, rows, bs):
    n = work.shape[0]
    for b in range(n // bs):
        lo = b * bs
        left = [work[lo + i:lo + i + 1, 0:n] for i in range(bs)]
        right = [work[lo + i:lo + i + 1, n:2 * n] for i in range(bs)]
        s = [[None] * bs for _ in range(bs)]
        for i in range(bs):
            for k in range(i + 1):
                s[i][k] = jnp.broadcast_to(left[i][:, lo + k:lo + k + 1], (1, n))
        scale = []
        for t in range(bs):
            inv = 1.0 / s[t][t]
            scale.append(lax.rsqrt(s[t][t]))
            fs = {i: s[i][t] * inv for i in range(t + 1, bs)}
            for i in range(t + 1, bs):
                for k in range(t + 1, i + 1):
                    s[i][k] = s[i][k] - (s[i][t] * s[k][t]) * inv
            for i in range(t + 1, bs):
                left[i] = left[i] - fs[i] * left[t]
                right[i] = right[i] - fs[i] * right[t]
        for i in range(bs):
            rows[lo + i:lo + i + 1, 0:n] = left[i] * scale[i]
            rows[lo + i:lo + i + 1, n:2 * n] = right[i] * scale[i]
        if lo + bs < n:
            blk = rows[lo:lo + bs, :]
            work[lo + bs:, :] = work[lo + bs:, :] - mm(blk[:, lo + bs:n], blk, TN)


def gj_inverse(work, bs):
    n = work.shape[0]
    for b in range(n // bs):
        lo = b * bs
        left = [work[lo + i:lo + i + 1, 0:n] for i in range(bs)]
        right = [work[lo + i:lo + i + 1, n:2 * n] for i in range(bs)]
        s = [[jnp.broadcast_to(left[i][:, lo + k:lo + k + 1], (1, n)) for k in range(bs)] for i in range(bs)]
        for t in range(bs):
            inv = 1.0 / s[t][t]
            for k in range(t + 1, bs):
                s[t][k] = s[t][k] * inv
            left[t] = left[t] * inv
            right[t] = right[t] * inv
            for i in range(bs):
                if i == t:
                    continue
                for k in range(t + 1, bs):
                    s[i][k] = s[i][k] - s[i][t] * s[t][k]
                left[i] = left[i] - s[i][t] * left[t]
                right[i] = right[i] - s[i][t] * right[t]
        lefts = jnp.concatenate(left, axis=0)
        rights = jnp.concatenate(right, axis=0)
        both = jnp.concatenate([lefts, rights], axis=1)
        cols = work[:, lo:lo + bs]
        rowi = lax.broadcasted_iota(jnp.int32, cols.shape, 0)
        cols = jnp.where((rowi >= lo) & (rowi < lo + bs), 0.0, cols)
        work[...] = work[...] - mm(cols, both)
        work[lo:lo + bs, :] = both


def place():
    row = lax.axis_index("row")
    return row // NZ, row % NZ, lax.axis_index("col")


def groups(ncol):
    x, z, c = place()
    gx = [(((x + d) % NX) * NZ + z, c) for d in range(NX)]
    gz = [(x * NZ + (z + d) % NZ, c) for d in range(NZ)]
    gc = [(x * NZ + z, (c + d) % ncol) for d in range(ncol)]
    return gx, gz, gc


def greet(ncol):
    sem = pltpu.get_barrier_semaphore()
    gx, gz, gc = groups(ncol)
    peers = gx[1:] + gz[1:] + gc[1:]
    for peer in peers:
        pl.semaphore_signal(sem, inc=1, device_id=peer, device_id_type=MESH)
    return sem, len(peers)


def send(src, dst, ss, rs, peer):
    copy = pltpu.make_async_remote_copy(
        src_ref=src, dst_ref=dst, send_sem=ss, recv_sem=rs, device_id=peer, device_id_type=MESH)
    copy.start()
    return copy


def slot_sum(buf, me, count):
    total = buf[me]
    for a in range(1, count):
        total = total + buf[(me + count - a) % count]
    return total


class Reduce:
    def __init__(self, out, xbuf, zbuf, sems, ncol):
        self.out, self.xbuf, self.zbuf, self.ncol = out, xbuf, zbuf, ncol
        self.xs, self.xr, self.zs, self.zr, self.cs, self.cr = sems
        self.gx, self.gz, self.gc = groups(ncol)
        self.x, self.z, self.c = place()
        self.sl = out.shape[0] // ncol
        self.open = []

    def part(self):
        return pl.ds(pl.multiple_of(self.c * self.sl, 8), self.sl)

    def start_x(self, src):
        self.xbuf[0] = src[self.part(), :]
        self.now = [send(self.xbuf.at[0], self.xbuf.at[d], self.xs.at[d], self.xr.at[d], self.gx[d]) for d in range(1, NX)]

    def start_z(self):
        for copy in self.now:
            copy.wait_recv()
        self.open += self.now
        self.zbuf[0] = slot_sum(self.xbuf, self.x, NX)
        self.now = [send(self.zbuf.at[0], self.zbuf.at[d], self.zs.at[d], self.zr.at[d], self.gz[d]) for d in range(1, NZ)]

    def start_c(self):
        for copy in self.now:
            copy.wait_recv()
        self.open += self.now
        self.out[self.part(), :] = slot_sum(self.zbuf, self.z, NZ)
        mine = self.out.at[self.part(), :]
        self.now = [send(mine, mine, self.cs.at[d], self.cr.at[d], self.gc[d]) for d in range(1, self.ncol)]

    def finish(self):
        for d, copy in enumerate(self.now, 1):
            rows = pl.ds(pl.multiple_of(((self.c + self.ncol - d) % self.ncol) * self.sl, 8), self.sl)
            theirs = self.out.at[rows, :]
            pltpu.make_async_remote_copy(
                src_ref=theirs, dst_ref=theirs, send_sem=self.cs.at[d], recv_sem=self.cr.at[d],
                device_id=self.gc[d], device_id_type=MESH).wait_recv()
        for copy in self.open + self.now:
            copy.wait_send()


def reduce_scratch(height, ncol):
    sl = height // ncol
    dma = pltpu.SemaphoreType.DMA
    return [pltpu.VMEM((NX, sl, 128), F32), pltpu.VMEM((NZ, sl, 128), F32),
            dma((NX,)), dma((NX,)), dma((NZ,)), dma((NZ,)), dma((ncol,)), dma((ncol,))]


VM = pl.BlockSpec(memory_space=pltpu.VMEM)
ANY = pl.BlockSpec(memory_space=pl.ANY)


def comm_params(cid):
    return pltpu.CompilerParams(collective_id=cid, has_side_effects=True, vmem_limit_bytes=60 << 20)


def first_kernel(ncol, p_ref, out_ref, src, xbuf, zbuf, *sems):
    sem, count = greet(ncol)
    p = p_ref[...]
    src[0:128, :] = mm(p, p, TN)
    lead = jnp.where(lax.axis_index("row") == 0, 1.0, 0.0)
    src[128:256, :] = p[0:128, :] * lead
    pl.semaphore_wait(sem, count)
    red = Reduce(out_ref, xbuf, zbuf, sems, ncol)
    red.start_x(src)
    red.start_z()
    red.start_c()
    red.finish()


def sum_kernel(ncol, a_ref, b_ref, out_ref, src, xbuf, zbuf, *sems):
    sem, count = greet(ncol)
    src[...] = mm(a_ref[...], b_ref[...], TN)
    pl.semaphore_wait(sem, count)
    red = Reduce(out_ref, xbuf, zbuf, sems, ncol)
    red.start_x(src)
    red.start_z()
    red.start_c()
    red.finish()


def chol_one(g_ref, l_ref, li_ref, xt_ref, work, rows):
    n = 128
    work[:, 0:n] = g_ref[0:n, :]
    work[:, n:] = jnp.where(eyes((n, n)), 1.0, 0.0)
    chol_inv(work, rows, 16)
    low = lax.broadcasted_iota(jnp.int32, (n, n), 0) >= lax.broadcasted_iota(jnp.int32, (n, n), 1)
    l_ref[...] = jnp.where(low, rows[:, 0:n].T, 0.0)
    inv = jnp.where(low, rows[:, n:], 0.0)
    li_ref[...] = inv
    xt_ref[...] = mm(g_ref[n:, :], inv, NT)


def second_kernel(ncol, p_ref, li_ref, p0, p1, p2, p3, a_ref,
                  g_ref, xr_ref, xc_ref, yw_ref,
                  src, xbuf, zbuf, xs, xr, zs, zr, cs, cr,
                  av, yp, ybuf, wbuf, asem, ys, yr, ws, wr, fs, fr):
    x, z, c = place()
    load = pltpu.make_async_copy(a_ref, av, asem)
    load.start()
    sem, count = greet(ncol)
    li = li_ref[...]
    first = mm(p_ref[...], li, NT)
    xr_ref[...] = first
    src[...] = mm(first, first, TN)
    pl.semaphore_wait(sem, count)
    red = Reduce(g_ref, xbuf, zbuf, (xs, xr, zs, zr, cs, cr), ncol)
    red.start_x(src)
    load.wait()
    sl = yp.shape[0] // ncol
    gc = red.gc

    def wsend(d):
        part = av.at[pl.ds(pl.multiple_of(d * sl, 8), sl), 0:128]
        return pltpu.make_async_remote_copy(
            src_ref=part, dst_ref=wbuf, send_sem=ws.at[d], recv_sem=wr,
            device_id=gc[d], device_id_type=MESH)

    parts = (p0, p1, p2, p3)

    def block(i):
        xi = mm(parts[i][...], li, NT)
        xc_ref[i] = xi
        width = xi.shape[0]
        at = pl.multiple_of(((x + i) % 4) * width, 128)
        return mm3(halves(av[:, pl.ds(at, width)]), halves(xi))

    acc = block(0)
    red.start_z()
    acc = acc + block(1)
    acc = acc + block(2)
    red.start_c()
    acc = acc + block(3)
    yp[...] = acc

    def mine(d):
        return pl.ds(pl.multiple_of(((c + d) % ncol) * sl, 8), sl)

    ybuf[0] = yp[mine(0), :]
    ysends = [send(yp.at[mine(d), :], ybuf.at[d], ys.at[d], yr.at[d], gc[d]) for d in range(1, ncol)]

    @pl.when(c == 0)
    def _():
        for d in range(1, ncol):
            wsend(d).start()
        wbuf[...] = av[0:sl, 0:128]

    red.finish()
    for copy in ysends:
        copy.wait_recv()

    @pl.when(c != 0)
    def _():
        wsend(1).wait_recv()

    yw_ref[mine(0), 0:128] = slot_sum(ybuf, c, ncol)
    yw_ref[mine(0), 128:256] = wbuf[...]
    own = yw_ref.at[mine(0), :]
    fsends = [send(own, own, fs.at[d], fr.at[d], gc[d]) for d in range(1, ncol)]
    for d in range(1, ncol):
        theirs = yw_ref.at[mine(ncol - d), :]
        pltpu.make_async_remote_copy(
            src_ref=theirs, dst_ref=theirs, send_sem=fs.at[d], recv_sem=fr.at[d],
            device_id=gc[d], device_id_type=MESH).wait_recv()
    for copy in ysends + fsends:
        copy.wait_send()

    @pl.when(c == 0)
    def _():
        for d in range(1, ncol):
            wsend(d).wait_send()


def chol_two(g_ref, l1_ref, xt_ref, xr_ref, yw_ref, rowi_ref, band_ref, l2i_ref, m_ref, v_ref, av_ref, work, rows):
    n = 128
    work[:, 0:n] = g_ref[...]
    work[:, n:] = jnp.where(eyes((n, n)), 1.0, 0.0)
    chol_inv(work, rows, 16)
    low = lax.broadcasted_iota(jnp.int32, (n, n), 0) >= lax.broadcasted_iota(jnp.int32, (n, n), 1)
    inv = jnp.where(low, rows[:, n:], 0.0)
    upper = jnp.where(low, rows[:, 0:n].T, 0.0).T
    av_ref[...] = mm(yw_ref[:, 0:n], inv, NT) + yw_ref[:, n:]
    ident = jnp.where(eyes(v_ref.shape, rowi_ref[0] * v_ref.shape[0]), 1.0, 0.0)
    v_ref[...] = mm(xr_ref[...], inv, NT) + ident
    l2i_ref[...] = inv
    band_ref[...] = -mm(upper, l1_ref[...], NT)
    top = mm(xt_ref[...], inv, NT)
    m_ref[...] = top.T + jnp.where(eyes((n, n)), 1.0, 0.0)


def inverse_kernel(m_ref, k_ref, work):
    n = 128
    work[:, 0:n] = m_ref[...]
    work[:, n:] = jnp.where(eyes((n, n)), 1.0, 0.0)
    gj_inverse(work, 8)
    k_ref[...] = work[:, n:]


def last_kernel(place_ref, k_ref, s_ref, l2i_ref, v_ref, avr_ref, xc_ref, q0, q1, q2, q3, a_ref, out_ref,
                abuf, obuf, vc, insem, outsem):
    n = 128
    width = q0.shape[0]

    def cols(i):
        return pl.ds(pl.multiple_of(((place_ref[0] + i) % 4) * width, 128), width)

    loads = [pltpu.make_async_copy(a_ref.at[:, cols(i)], abuf.at[i], insem.at[i]) for i in range(4)]
    for copy in loads:
        copy.start()
    k = k_ref[...]
    inner = mm(k, mm(s_ref[...], k), TN)
    both = -0.5 * (inner + inner.T)
    right = jnp.concatenate([
        jnp.concatenate([jnp.zeros((n, n), F32), k], axis=1),
        jnp.concatenate([k.T, both], axis=1)], axis=0)
    pair = jnp.concatenate([avr_ref[...], v_ref[...]], axis=1)
    lead = halves(mm(pair, right))
    stores = []
    for i, q in enumerate((q0, q1, q2, q3)):
        shift = (place_ref[1] * 4 + (place_ref[0] + i) % 4) * width
        vi = mm(xc_ref[i], l2i_ref[...], NT) + jnp.where(eyes((width, n), shift), 1.0, 0.0)
        tail = halves(jnp.concatenate([q[...], vi], axis=1))
        prod = mm3(lead, tail, NT)
        loads[i].wait()
        obuf[i] = abuf[i] - prod
        copy = pltpu.make_async_copy(obuf.at[i], out_ref.at[:, cols(i)], outsem.at[i])
        copy.start()
        stores.append(copy)
    for copy in stores:
        copy.wait()


def struct(*shape):
    return jax.ShapeDtypeStruct(shape, F32)


def spread(block, nrow, ncol):
    out = []
    for i in range(4):
        perm = []
        for xq in range(NX):
            for zq in range(NZ):
                for cq in range(ncol):
                    core, k = zq // 4, zq % 4
                    xd = (k - i) % 4
                    perm.append(((xq * NZ + zq) * ncol + cq, (xd * NZ + cq) * ncol + xq * 2 + core))
        out.append(lax.ppermute(block, ("row", "col"), perm))
    return out


def body(nrow, ncol, panel, trailing):
    n = panel.shape[1]
    height, width = trailing.shape
    row = lax.axis_index("row")
    col = lax.axis_index("col")
    pc = spread(panel, nrow, ncol)

    gt = pl.pallas_call(
        functools.partial(first_kernel, ncol), out_shape=struct(2 * n, n), in_specs=[VM], out_specs=VM,
        scratch_shapes=[pltpu.VMEM((2 * n, n), F32)] + reduce_scratch(2 * n, ncol),
        compiler_params=comm_params(0))(panel)

    wide = pltpu.VMEM((n, 2 * n), F32)
    l1, l1i, xt = pl.pallas_call(
        chol_one, out_shape=(struct(n, n),) * 3, in_specs=[VM], out_specs=(VM,) * 3,
        scratch_shapes=[wide, wide])(gt)

    dma = pltpu.SemaphoreType.DMA
    sl = height // ncol
    g2, xr, xc, yw = pl.pallas_call(
        functools.partial(second_kernel, ncol),
        out_shape=(struct(n, n), struct(height, n), struct(4, height, n), struct(height, 2 * n)),
        in_specs=[VM] * 6 + [ANY], out_specs=(VM,) * 4,
        scratch_shapes=[pltpu.VMEM((n, n), F32)] + reduce_scratch(n, ncol) + [
            pltpu.VMEM((height, width), F32), pltpu.VMEM((height, n), F32),
            pltpu.VMEM((ncol, sl, n), F32), pltpu.VMEM((sl, n), F32), dma,
            dma((ncol,)), dma((ncol,)), dma((ncol,)), dma, dma((ncol,)), dma((ncol,))],
        compiler_params=comm_params(1))(panel, l1i, *pc, trailing)

    SM = pl.BlockSpec(memory_space=pltpu.SMEM)
    band, l2i, m, v, av = pl.pallas_call(
        chol_two, out_shape=(struct(n, n), struct(n, n), struct(n, n), struct(height, n), struct(height, n)),
        in_specs=[VM] * 5 + [SM], out_specs=(VM,) * 5,
        scratch_shapes=[wide, wide])(g2, l1, xt, xr, yw, row[None])

    qc = spread(av, nrow, ncol)
    s = pl.pallas_call(
        functools.partial(sum_kernel, ncol), out_shape=struct(n, n), in_specs=[VM] * 2, out_specs=VM,
        scratch_shapes=[pltpu.VMEM((n, n), F32)] + reduce_scratch(n, ncol),
        compiler_params=comm_params(2))(v, av)
    k = pl.pallas_call(
        inverse_kernel, out_shape=struct(n, n), in_specs=[VM], out_specs=VM, scratch_shapes=[wide])(m)

    where = jnp.stack([row // NZ, col])
    reduced = pl.pallas_call(
        last_kernel, out_shape=struct(height, width),
        in_specs=[SM] + [VM] * 10 + [ANY], out_specs=ANY,
        scratch_shapes=[pltpu.VMEM((4, height, width // 4), F32)] * 2 + [
            pltpu.VMEM((height, n), F32), dma((4,)), dma((4,))],
        compiler_params=pltpu.CompilerParams(vmem_limit_bytes=60 << 20),
    )(where, k, s, l2i, v, av, xc, *qc, trailing)
    return reduced, band, l1


def solution(mesh):
    nrow, ncol = mesh.shape["row"], mesh.shape["col"]
    return jax.shard_map(
        functools.partial(body, nrow, ncol), mesh=mesh, in_specs=(P("row", None), P("row", "col")),
        out_specs=(P("row", "col"), P(), P()), check_vma=False)
```

```python
import functools

import jax
import jax.numpy as jnp
from jax import lax
from jax.experimental import pallas as pl
from jax.experimental.pallas import tpu as pltpu
from jax.sharding import PartitionSpec as P

HIGH = lax.Precision.HIGHEST
F32 = jnp.float32
BF16 = jnp.bfloat16
MESH = pl.DeviceIdType.MESH
NX, NZ = 4, 8
BS = 16
NN = (((1,), (0,)), ((), ()))
NT = (((1,), (1,)), ((), ()))
TN = (((0,), (0,)), ((), ()))


def mm(a, b, dims=NN):
    return lax.dot_general(a, b, dims, precision=HIGH, preferred_element_type=F32)


def halves(a):
    top = a.astype(BF16)
    return top, (a - top.astype(F32)).astype(BF16)


def mm3(a, b, dims=NN):
    def one(p, q):
        return lax.dot_general(p, q, dims, preferred_element_type=F32)
    return one(a[0], b[0]) + (one(a[0], b[1]) + one(a[1], b[0]))


def eyes(shape, shift=0):
    return (lax.broadcasted_iota(jnp.int32, shape, 0) + shift) == lax.broadcasted_iota(jnp.int32, shape, 1)


def over(row, count):
    return jnp.broadcast_to(row, (count, row.shape[1]))


def eliminate(work, lo, hot, jordan):
    n = work.shape[0]
    bs = len(hot)
    rows = work[lo:lo + bs, :]
    col = [jnp.broadcast_to(rows[:, lo + k:lo + k + 1], (bs, n)) for k in range(bs)]
    pivots = []
    left, right = rows[:, 0:n], rows[:, n:]
    for t in range(bs):
        pivot = over(col[t][t:t + 1, :], bs)
        pivots.append(pivot[0:1, :])
        inv = 1.0 / pivot
        f = col[t] - hot[t] if jordan else jnp.where(hot[t], col[t], 0.0)
        for k in range(t + 1, bs):
            col[k] = col[k] - (f * over(col[k][t:t + 1, :], bs)) * inv
        g = f * inv
        left = left - g * over(left[t:t + 1, :], bs)
        right = right - g * over(right[t:t + 1, :], bs)
    return left, right, pivots


def chol_inv(work, rows, hooks=()):
    n = work.shape[0]
    at = lax.broadcasted_iota(jnp.int32, (BS, n), 0)
    hot = [at > t for t in range(BS)]
    for b in range(n // BS):
        lo = b * BS
        left, right, pivots = eliminate(work, lo, hot, False)
        scale = lax.rsqrt(jnp.concatenate(pivots, axis=0))
        blk = jnp.concatenate([left * scale, right * scale], axis=1)
        rows[lo:lo + BS, :] = blk
        if lo + BS < n:
            work[lo + BS:, :] = work[lo + BS:, :] - mm(blk[:, lo + BS:n], blk, TN)
        if b in hooks:
            hooks[b]()


def gj_inverse(work, hooks=()):
    n = work.shape[0]
    at = lax.broadcasted_iota(jnp.int32, (BS, n), 0)
    hot = [jnp.where(at == t, 1.0, 0.0) for t in range(BS)]
    for b in range(n // BS):
        lo = b * BS
        left, right, _ = eliminate(work, lo, hot, True)
        both = jnp.concatenate([left, right], axis=1)
        cols = work[:, lo:lo + BS]
        rowi = lax.broadcasted_iota(jnp.int32, cols.shape, 0)
        cols = jnp.where((rowi >= lo) & (rowi < lo + BS), 0.0, cols)
        work[...] = work[...] - mm(cols, both)
        work[lo:lo + BS, :] = both
        if b in hooks:
            hooks[b]()


def with_identity(work, square):
    n = work.shape[0]
    work[:, 0:n] = square
    work[:, n:] = jnp.where(eyes((n, n)), 1.0, 0.0)


def factors(rows):
    n = rows.shape[0]
    low = lax.broadcasted_iota(jnp.int32, (n, n), 0) >= lax.broadcasted_iota(jnp.int32, (n, n), 1)
    return jnp.where(low, rows[:, 0:n].T, 0.0), jnp.where(low, rows[:, n:], 0.0)


def place():
    row = lax.axis_index("row")
    return row // NZ, row % NZ, lax.axis_index("col")


def groups(ncol):
    x, z, c = place()
    gx = [(((x + d) % NX) * NZ + z, c) for d in range(NX)]
    gz = [(x * NZ + (z + d) % NZ, c) for d in range(NZ)]
    gc = [(x * NZ + z, (c + d) % ncol) for d in range(ncol)]
    return gx, gz, gc


def greet(ncol):
    sem = pltpu.get_barrier_semaphore()
    gx, gz, gc = groups(ncol)
    peers = gx[1:] + gz[1:] + gc[1:]
    for peer in peers:
        pl.semaphore_signal(sem, inc=1, device_id=peer, device_id_type=MESH)
    return sem, len(peers)


def send(src, dst, ss, rs, peer):
    copy = pltpu.make_async_remote_copy(
        src_ref=src, dst_ref=dst, send_sem=ss, recv_sem=rs, device_id=peer, device_id_type=MESH)
    copy.start()
    return copy


def slot_sum(buf, me, count):
    total = buf[me]
    for a in range(1, count):
        total = total + buf[(me + count - a) % count]
    return total


class Reduce:
    def __init__(self, out, xbuf, zbuf, sems, ncol):
        self.out, self.xbuf, self.zbuf, self.ncol = out, xbuf, zbuf, ncol
        self.xs, self.xr, self.zs, self.zr, self.cs, self.cr = sems
        self.gx, self.gz, self.gc = groups(ncol)
        self.x, self.z, self.c = place()
        self.sl = out.shape[0] // ncol
        self.open = []

    def part(self):
        return pl.ds(pl.multiple_of(self.c * self.sl, 8), self.sl)

    def start_x(self, src):
        self.xbuf[0] = src[self.part(), :]
        self.now = [send(self.xbuf.at[0], self.xbuf.at[d], self.xs.at[d], self.xr.at[d], self.gx[d]) for d in range(1, NX)]

    def start_z(self):
        for copy in self.now:
            copy.wait_recv()
        self.open += self.now
        self.zbuf[0] = slot_sum(self.xbuf, self.x, NX)
        self.now = [send(self.zbuf.at[0], self.zbuf.at[d], self.zs.at[d], self.zr.at[d], self.gz[d]) for d in range(1, NZ)]

    def start_c(self):
        for copy in self.now:
            copy.wait_recv()
        self.open += self.now
        self.out[self.part(), :] = slot_sum(self.zbuf, self.z, NZ)
        mine = self.out.at[self.part(), :]
        self.now = [send(mine, mine, self.cs.at[d], self.cr.at[d], self.gc[d]) for d in range(1, self.ncol)]

    def finish(self):
        for d, copy in enumerate(self.now, 1):
            rows = pl.ds(pl.multiple_of(((self.c + self.ncol - d) % self.ncol) * self.sl, 8), self.sl)
            theirs = self.out.at[rows, :]
            pltpu.make_async_remote_copy(
                src_ref=theirs, dst_ref=theirs, send_sem=self.cs.at[d], recv_sem=self.cr.at[d],
                device_id=self.gc[d], device_id_type=MESH).wait_recv()
        for copy in self.open + self.now:
            copy.wait_send()


def reduce_scratch(height, ncol):
    sl = height // ncol
    dma = pltpu.SemaphoreType.DMA
    return [pltpu.VMEM((NX, sl, 128), F32), pltpu.VMEM((NZ, sl, 128), F32),
            dma((NX,)), dma((NX,)), dma((NZ,)), dma((NZ,)), dma((ncol,)), dma((ncol,))]


VM = pl.BlockSpec(memory_space=pltpu.VMEM)
ANY = pl.BlockSpec(memory_space=pl.ANY)


def comm_params(cid):
    return pltpu.CompilerParams(collective_id=cid, has_side_effects=True, vmem_limit_bytes=60 << 20)


def turn(y):
    return (y + 2) % 3 + y // 3


def unturn(t):
    return (t + 1) % 3 * (1 - t // 3) + 3 * (t // 3)


class Gather:
    def __init__(self, src, out, sems, ncol):
        self.src, self.out = src, out
        self.s1, self.r1, self.s2, self.r2 = sems
        self.x, self.z, self.c = place()
        y, core = self.c // 2, self.c % 2
        self.quarter = src.shape[0] // NX
        xd = (turn(y) + NX - self.x) % NX
        self.xd = xd
        self.to = [((xd * NZ) + 2 * j + core, self.x * 2 + self.z // 4) for j in range(4)]
        ys = unturn((self.x + y) % NX)
        self.frm = [(y * NZ + 4 * core + k, ys * 2 + self.z % 2) for k in range(4)]
        self.gx = groups(ncol)[0]

    def rows(self, x):
        return pl.ds(pl.multiple_of(x * self.quarter, 128), self.quarter)

    def start_one(self):
        k = self.z % 4
        self.one = [send(self.src.at[self.rows(self.xd), :], self.out.at[k, self.rows(self.xd), :],
                         self.s1.at[j], self.r1.at[k], self.to[j]) for j in range(4)]

    def start_two(self):
        self.two = []
        for j in range(4):
            k = (self.z + j) % 4
            part = self.out.at[k, self.rows(self.x), :]
            pltpu.make_async_remote_copy(
                src_ref=part, dst_ref=part, send_sem=self.s1.at[j], recv_sem=self.r1.at[k],
                device_id=self.frm[0], device_id_type=MESH).wait_recv()
            self.two += [send(part, part, self.s2.at[d, j], self.r2.at[d, k], self.gx[d]) for d in range(1, NX)]

    def block(self, k):
        for d in range(1, NX):
            part = self.out.at[k, self.rows((self.x + NX - d) % NX), :]
            pltpu.make_async_remote_copy(
                src_ref=part, dst_ref=part, send_sem=self.s2.at[d, k], recv_sem=self.r2.at[d, k],
                device_id=self.gx[d], device_id_type=MESH).wait_recv()

    def finish(self):
        for copy in self.one + self.two:
            copy.wait_send()


def gather_sems():
    dma = pltpu.SemaphoreType.DMA
    return [dma((4,)), dma((4,)), dma((NX, 4)), dma((NX, 4))]


VM = pl.BlockSpec(memory_space=pltpu.VMEM)
ANY = pl.BlockSpec(memory_space=pl.ANY)


def struct(*shape):
    return jax.ShapeDtypeStruct(shape, F32)


def main_kernel(ncol, p_ref, a_ref, l1_ref, band_ref, lead_ref, avc_ref, vc_ref, *scratch):
    scratch = list(scratch)

    def take(count):
        head = scratch[:count]
        del scratch[:count]
        return head

    src1, out1, src2, out2, src3, out3 = take(6)
    red1, red2, red3 = take(8), take(8), take(8)
    gs1, gs2 = take(4), take(4)
    av, pc, work, rows, yp, ybuf, wbuf, yw, avr = take(9)
    asem, ys, yr, ws, wr, fs, fr = take(7)
    n = p_ref.shape[1]
    height = p_ref.shape[0]
    row, c = lax.axis_index("row"), lax.axis_index("col")

    load = pltpu.make_async_copy(a_ref, av, asem)
    load.start()
    sem, count = greet(ncol)
    early = Gather(p_ref, pc, gs1, ncol)
    late = Gather(avr, avc_ref, gs2, ncol)
    for peer in early.to + early.frm:
        pl.semaphore_signal(sem, inc=1, device_id=peer, device_id_type=MESH)
    count += len(early.to) + len(early.frm)
    p = p_ref[...]
    src1[0:n, :] = mm(p, p, TN)
    src1[n:, :] = p[0:n, :] * jnp.where(row == 0, 1.0, 0.0)
    pl.semaphore_wait(sem, count)

    red = Reduce(out1, red1[0], red1[1], red1[2:], ncol)
    red.start_x(src1)
    early.start_one()
    red.start_z()
    red.start_c()
    early.start_two()
    red.finish()
    with_identity(work, out1[0:n, :])
    chol_inv(work, rows)
    l1, l1i = factors(rows)
    l1_ref[...] = l1

    xr = mm(p_ref[...], l1i, NT)
    src2[...] = mm(xr, xr, TN)
    red = Reduce(out2, red2[0], red2[1], red2[2:], ncol)
    red.start_x(src2)
    lead_ref[:, 0:n] = xr
    xt = mm(out1[n:, :], l1i, NT)
    load.wait()
    red.start_z()

    def block(k):
        early.block(k)
        xk = mm(pc[k], l1i, NT)
        vc_ref[k] = xk
        return mm3(halves(av[:, k * height:(k + 1) * height]), halves(xk))

    acc = block(0)
    acc = acc + block(1)
    red.start_c()
    acc = acc + block(2)
    acc = acc + block(3)
    yp[...] = acc
    early.finish()
    sl = height // ncol
    gc = red.gc

    def part(d):
        return pl.ds(pl.multiple_of(((c + d) % ncol) * sl, 8), sl)

    def wsend(d):
        return pltpu.make_async_remote_copy(
            src_ref=av.at[d * sl:(d + 1) * sl, 0:n], dst_ref=wbuf, send_sem=ws.at[d], recv_sem=wr,
            device_id=gc[d], device_id_type=MESH)

    ybuf[0] = yp[part(0), :]
    ysends = [send(yp.at[part(d), :], ybuf.at[d], ys.at[d], yr.at[d], gc[d]) for d in range(1, ncol)]

    @pl.when(c == 0)
    def _():
        for d in range(1, ncol):
            wsend(d).start()
        wbuf[...] = av[0:sl, 0:n]

    red.finish()
    fsends = []

    def share():
        for copy in ysends:
            copy.wait_recv()

        @pl.when(c != 0)
        def _():
            wsend(1).wait_recv()

        yw[part(0), 0:n] = slot_sum(ybuf, c, ncol)
        yw[part(0), n:] = wbuf[...]
        own = yw.at[part(0), :]
        fsends.extend(send(own, own, fs.at[d], fr.at[d], gc[d]) for d in range(1, ncol))

    with_identity(work, out2[...])
    chol_inv(work, rows, {4: share})
    l2, l2i = factors(rows)
    for d in range(1, ncol):
        theirs = yw.at[part(ncol - d), :]
        pltpu.make_async_remote_copy(
            src_ref=theirs, dst_ref=theirs, send_sem=fs.at[d], recv_sem=fr.at[d],
            device_id=gc[d], device_id_type=MESH).wait_recv()

    avr[...] = mm(yw[:, 0:n], l2i, NT) + yw[:, n:]
    late.start_one()
    vr = mm(lead_ref[:, 0:n], l2i, NT) + jnp.where(eyes((height, n), row * height), 1.0, 0.0)
    src3[...] = mm(vr, avr[...], TN)
    red = Reduce(out3, red3[0], red3[1], red3[2:], ncol)
    red.start_x(src3)
    with_identity(work, mm(xt, l2i, NT).T + jnp.where(eyes((n, n)), 1.0, 0.0))
    gj_inverse(work, {3: red.start_z})
    k = work[:, n:]
    red.start_c()
    late.start_two()
    for j in range(4):
        shift = (c * 4 + j) * height
        vc_ref[j] = mm(vc_ref[j], l2i, NT) + jnp.where(eyes((height, n), shift), 1.0, 0.0)
    band_ref[...] = -mm(l2, l1_ref[...], (((0,), (1,)), ((), ())))
    red.finish()
    inner = mm(k, mm(out3[...], k), TN)
    right = jnp.concatenate([
        jnp.concatenate([jnp.zeros((n, n), F32), k], axis=1),
        jnp.concatenate([k.T, -0.5 * (inner + inner.T)], axis=1)], axis=0)
    lead_ref[...] = mm(jnp.concatenate([avr[...], vr], axis=1), right)
    for j in range(4):
        late.block(j)
    late.finish()
    for copy in ysends + fsends:
        copy.wait_send()

    @pl.when(c == 0)
    def _():
        for d in range(1, ncol):
            wsend(d).wait_send()


def last_kernel(l1_in, band_in, lead_ref, avc_ref, vc_ref, a_ref, out_ref, band_ref, l1_ref, abuf, obuf, insem, outsem):
    width = avc_ref.shape[1]
    loads = [pltpu.make_async_copy(a_ref.at[:, k * width:(k + 1) * width], abuf.at[k], insem.at[k]) for k in range(4)]
    for copy in loads:
        copy.start()
    band_ref[...] = band_in[...]
    l1_ref[...] = l1_in[...]
    lead = halves(lead_ref[...])
    stores = []
    for k in range(4):
        tail = halves(jnp.concatenate([avc_ref[k], vc_ref[k]], axis=1))
        prod = mm3(lead, tail, NT)
        loads[k].wait()
        obuf[k] = abuf[k] - prod
        copy = pltpu.make_async_copy(obuf.at[k], out_ref.at[:, k * width:(k + 1) * width], outsem.at[k])
        copy.start()
        stores.append(copy)
    for copy in stores:
        copy.wait()


def body(ncol, panel, trailing):
    n = panel.shape[1]
    height, width = trailing.shape
    sl = height // ncol
    dma = pltpu.SemaphoreType.DMA

    def vmem(*shape):
        return pltpu.VMEM(shape, F32)

    l1, band, lead, avc, vc = pl.pallas_call(
        functools.partial(main_kernel, ncol),
        out_shape=(struct(n, n), struct(n, n), struct(height, 2 * n), struct(4, height, n), struct(4, height, n)),
        in_specs=[VM, ANY], out_specs=(VM,) * 5,
        scratch_shapes=[vmem(2 * n, n), vmem(2 * n, n), vmem(n, n), vmem(n, n), vmem(n, n), vmem(n, n)]
        + reduce_scratch(2 * n, ncol) + reduce_scratch(n, ncol) + reduce_scratch(n, ncol)
        + gather_sems() + gather_sems()
        + [vmem(height, width), vmem(4, height, n), vmem(n, 2 * n), vmem(n, 2 * n), vmem(height, n),
           vmem(ncol, sl, n), vmem(sl, n), vmem(height, 2 * n), vmem(height, n)]
        + [dma, dma((ncol,)), dma((ncol,)), dma((ncol,)), dma, dma((ncol,)), dma((ncol,))],
        compiler_params=pltpu.CompilerParams(collective_id=0, has_side_effects=True, vmem_limit_bytes=60 << 20),
        name="main")(panel, trailing)
    reduced, band, l1 = pl.pallas_call(
        last_kernel, out_shape=(struct(height, width), struct(n, n), struct(n, n)),
        in_specs=[VM] * 5 + [ANY], out_specs=(ANY, VM, VM),
        scratch_shapes=[vmem(4, height, width // 4), vmem(4, height, width // 4), dma((4,)), dma((4,))],
        compiler_params=pltpu.CompilerParams(vmem_limit_bytes=60 << 20), name="last",
    )(l1, band, lead, avc, vc, trailing)
    return reduced, band, l1


def solution(mesh):
    return jax.shard_map(
        functools.partial(body, mesh.shape["col"]), mesh=mesh, in_specs=(P("row", None), P("row", "col")),
        out_specs=(P("row", "col"), P(), P()), check_vma=False)
```

```python
import functools

import jax
import jax.numpy as jnp
from jax import lax
from jax.experimental import pallas as pl
from jax.experimental.pallas import tpu as pltpu
from jax.sharding import PartitionSpec as P

HIGH = lax.Precision.HIGHEST
F32 = jnp.float32
BF16 = jnp.bfloat16
MESH = pl.DeviceIdType.MESH
NX, NZ = 4, 8
BS = 16
NN = (((1,), (0,)), ((), ()))
NT = (((1,), (1,)), ((), ()))
TN = (((0,), (0,)), ((), ()))


def mm(a, b, dims=NN):
    return lax.dot_general(a, b, dims, precision=HIGH, preferred_element_type=F32)


def halves(a):
    top = a.astype(BF16)
    return top, (a - top.astype(F32)).astype(BF16)


def mm3(a, b, dims=NN):
    def one(p, q):
        return lax.dot_general(p, q, dims, preferred_element_type=F32)
    return one(a[0], b[0]) + (one(a[0], b[1]) + one(a[1], b[0]))


def eyes(shape, shift=0):
    return (lax.broadcasted_iota(jnp.int32, shape, 0) + shift) == lax.broadcasted_iota(jnp.int32, shape, 1)


def over(row, count):
    return jnp.broadcast_to(row, (count, row.shape[1]))


def eliminate(work, lo, hot, jordan):
    n = work.shape[0]
    bs = len(hot)
    rows = work[lo:lo + bs, :]
    col = [jnp.broadcast_to(rows[:, lo + k:lo + k + 1], (bs, n)) for k in range(bs)]
    pivots = []
    left, right = rows[:, 0:n], rows[:, n:]
    for t in range(bs):
        pivot = over(col[t][t:t + 1, :], bs)
        pivots.append(pivot[0:1, :])
        inv = 1.0 / pivot
        f = col[t] - hot[t] if jordan else jnp.where(hot[t], col[t], 0.0)
        for k in range(t + 1, bs):
            col[k] = col[k] - (f * over(col[k][t:t + 1, :], bs)) * inv
        g = f * inv
        left = left - g * over(left[t:t + 1, :], bs)
        right = right - g * over(right[t:t + 1, :], bs)
    return left, right, pivots


def chol_inv(work, rows, hooks=()):
    n = work.shape[0]
    at = lax.broadcasted_iota(jnp.int32, (BS, n), 0)
    hot = [at > t for t in range(BS)]
    for b in range(n // BS):
        lo = b * BS
        left, right, pivots = eliminate(work, lo, hot, False)
        scale = lax.rsqrt(jnp.concatenate(pivots, axis=0))
        blk = jnp.concatenate([left * scale, right * scale], axis=1)
        rows[lo:lo + BS, :] = blk
        if lo + BS < n:
            work[lo + BS:, :] = work[lo + BS:, :] - mm(blk[:, lo + BS:n], blk, TN)
        if b in hooks:
            hooks[b]()


def gj_inverse(work, hooks=()):
    n = work.shape[0]
    at = lax.broadcasted_iota(jnp.int32, (BS, n), 0)
    hot = [jnp.where(at == t, 1.0, 0.0) for t in range(BS)]
    for b in range(n // BS):
        lo = b * BS
        left, right, _ = eliminate(work, lo, hot, True)
        both = jnp.concatenate([left, right], axis=1)
        cols = work[:, lo:lo + BS]
        rowi = lax.broadcasted_iota(jnp.int32, cols.shape, 0)
        cols = jnp.where((rowi >= lo) & (rowi < lo + BS), 0.0, cols)
        work[...] = work[...] - mm(cols, both)
        work[lo:lo + BS, :] = both
        if b in hooks:
            hooks[b]()


def with_identity(work, square):
    n = work.shape[0]
    work[:, 0:n] = square
    work[:, n:] = jnp.where(eyes((n, n)), 1.0, 0.0)


def factors(rows):
    n = rows.shape[0]
    low = lax.broadcasted_iota(jnp.int32, (n, n), 0) >= lax.broadcasted_iota(jnp.int32, (n, n), 1)
    return jnp.where(low, rows[:, 0:n].T, 0.0), jnp.where(low, rows[:, n:], 0.0)


def place():
    row = lax.axis_index("row")
    return row // NZ, row % NZ, lax.axis_index("col")


def groups(ncol):
    x, z, c = place()
    gx = [(((x + d) % NX) * NZ + z, c) for d in range(NX)]
    gz = [(x * NZ + (z + d) % NZ, c) for d in range(NZ)]
    gc = [(x * NZ + z, (c + d) % ncol) for d in range(ncol)]
    return gx, gz, gc


def greet(ncol):
    sem = pltpu.get_barrier_semaphore()
    gx, gz, gc = groups(ncol)
    peers = gx[1:] + gz[1:] + gc[1:]
    for peer in peers:
        pl.semaphore_signal(sem, inc=1, device_id=peer, device_id_type=MESH)
    return sem, len(peers)


def send(src, dst, ss, rs, peer):
    copy = pltpu.make_async_remote_copy(
        src_ref=src, dst_ref=dst, send_sem=ss, recv_sem=rs, device_id=peer, device_id_type=MESH)
    copy.start()
    return copy


def slot_sum(buf, me, count):
    total = buf[me]
    for a in range(1, count):
        total = total + buf[(me + count - a) % count]
    return total


class Reduce:
    def __init__(self, out, xbuf, zbuf, sems, ncol):
        self.out, self.xbuf, self.zbuf, self.ncol = out, xbuf, zbuf, ncol
        self.xs, self.xr, self.zs, self.zr, self.cs, self.cr = sems
        self.gx, self.gz, self.gc = groups(ncol)
        self.x, self.z, self.c = place()
        self.sl = out.shape[0] // ncol
        self.open = []

    def part(self):
        return pl.ds(pl.multiple_of(self.c * self.sl, 8), self.sl)

    def start_x(self, src):
        self.xbuf[0] = src[self.part(), :]
        self.now = [send(self.xbuf.at[0], self.xbuf.at[d], self.xs.at[d], self.xr.at[d], self.gx[d]) for d in range(1, NX)]

    def start_z(self):
        for copy in self.now:
            copy.wait_recv()
        self.open += self.now
        self.zbuf[0] = slot_sum(self.xbuf, self.x, NX)
        self.now = [send(self.zbuf.at[0], self.zbuf.at[d], self.zs.at[d], self.zr.at[d], self.gz[d]) for d in range(1, NZ)]

    def start_c(self):
        for copy in self.now:
            copy.wait_recv()
        self.open += self.now
        self.out[self.part(), :] = slot_sum(self.zbuf, self.z, NZ)
        mine = self.out.at[self.part(), :]
        self.now = [send(mine, mine, self.cs.at[d], self.cr.at[d], self.gc[d]) for d in range(1, self.ncol)]

    def finish(self):
        for d, copy in enumerate(self.now, 1):
            rows = pl.ds(pl.multiple_of(((self.c + self.ncol - d) % self.ncol) * self.sl, 8), self.sl)
            theirs = self.out.at[rows, :]
            pltpu.make_async_remote_copy(
                src_ref=theirs, dst_ref=theirs, send_sem=self.cs.at[d], recv_sem=self.cr.at[d],
                device_id=self.gc[d], device_id_type=MESH).wait_recv()
        for copy in self.open + self.now:
            copy.wait_send()


def reduce_scratch(height, ncol):
    sl = height // ncol
    dma = pltpu.SemaphoreType.DMA
    return [pltpu.VMEM((NX, sl, 128), F32), pltpu.VMEM((NZ, sl, 128), F32),
            dma((NX,)), dma((NX,)), dma((NZ,)), dma((NZ,)), dma((ncol,)), dma((ncol,))]


VM = pl.BlockSpec(memory_space=pltpu.VMEM)
ANY = pl.BlockSpec(memory_space=pl.ANY)


def comm_params(cid):
    return pltpu.CompilerParams(collective_id=cid, has_side_effects=True, vmem_limit_bytes=60 << 20)


def turn(y):
    return (y + 2) % 3 + y // 3


def unturn(t):
    return (t + 1) % 3 * (1 - t // 3) + 3 * (t // 3)


class Gather:
    def __init__(self, src, out, sems, ncol):
        self.src, self.out = src, out
        self.s1, self.r1, self.s2, self.r2, self.s3, self.r3 = sems
        self.two = []
        self.x, self.z, self.c = place()
        y, core = self.c // 2, self.c % 2
        self.quarter = src.shape[0] // NX
        xd = (turn(y) + NX - self.x) % NX
        self.xd = xd
        self.to = [((xd * NZ) + 2 * j + core, self.x * 2 + self.z // 4) for j in range(4)]
        ys = unturn((self.x + y) % NX)
        self.frm = [(y * NZ + 4 * core + k, ys * 2 + self.z % 2) for k in range(4)]
        self.gx = groups(ncol)[0]

    def rows(self, x):
        return pl.ds(pl.multiple_of(x * self.quarter, 128), self.quarter)

    def start_one(self):
        k = self.z % 4
        self.one = [send(self.src.at[self.rows(self.xd), :], self.out.at[k, self.rows(self.xd), :],
                         self.s1.at[j], self.r1.at[k], self.to[j]) for j in range(4)]

    def arrived(self, x, k, sem, lo=0, count=None):
        rows = self.rows(x) if count is None else pl.ds(pl.multiple_of(x * self.quarter + lo, 8), count)
        part = self.out.at[k, rows, :]
        pltpu.make_async_remote_copy(
            src_ref=part, dst_ref=part, send_sem=self.s1.at[0], recv_sem=sem,
            device_id=self.frm[0], device_id_type=MESH).wait_recv()
        return part

    def nearest(self, j):
        return (self.z + j) % 4

    def forward(self, j, steps=(1, 2, 3)):
        k = self.nearest(j)
        part = self.arrived(self.x, k, self.r1.at[k])
        self.two += [send(part, part, self.s2.at[d, j], self.r2.at[d, k], self.gx[d]) for d in steps]

    def relay(self, j):
        k = self.nearest(j)
        half = self.quarter // 2
        for i, d in enumerate((1, 3)):
            x = (self.x + NX - d) % NX
            self.arrived(x, k, self.r2.at[d, k])
            part = self.out.at[k, pl.ds(pl.multiple_of(x * self.quarter + i * half, 8), half), :]
            self.two.append(send(part, part, self.s3.at[i, j], self.r3.at[i, k], self.gx[d]))

    def block(self, k):
        for d in range(1, NX):
            self.arrived((self.x + NX - d) % NX, k, self.r2.at[d, k])

    def relayed(self, k):
        half = self.quarter // 2
        for i in range(2):
            self.arrived((self.x + 2) % NX, k, self.r3.at[i, k], i * half, half)

    def finish(self):
        for copy in self.one + self.two:
            copy.wait_send()


def gather_sems():
    dma = pltpu.SemaphoreType.DMA
    return [dma((4,)), dma((4,)), dma((NX, 4)), dma((NX, 4)), dma((2, 4)), dma((2, 4))]


VM = pl.BlockSpec(memory_space=pltpu.VMEM)
ANY = pl.BlockSpec(memory_space=pl.ANY)


def struct(*shape):
    return jax.ShapeDtypeStruct(shape, F32)


def main_kernel(ncol, p_hbm, a_ref, l1_out, band_out, lead_out, avc_out, vc_out, *scratch):
    scratch = list(scratch)

    def take(count):
        head = scratch[:count]
        del scratch[:count]
        return head

    src1, out1, src2, out2, src3, out3 = take(6)
    red1, red2, red3 = take(8), take(8), take(8)
    gs1, gs2 = take(6), take(6)
    av, pc, work, rows, yp, ybuf, wbuf, yw, avr = take(9)
    p_ref, l1_ref, band_ref, lead_ref, avc_ref, vc_ref = take(6)
    asem, psem, osem, ys, yr, ws, wr, vs, vr_sem, fs, fr = take(11)
    n = p_ref.shape[1]
    height = p_ref.shape[0]
    sl = height // ncol
    row, c = lax.axis_index("row"), lax.axis_index("col")

    sem, count = greet(ncol)
    early = Gather(p_ref, pc, gs1, ncol)
    late = Gather(avr, avc_ref, gs2, ncol)
    for peer in early.to + early.frm:
        pl.semaphore_signal(sem, inc=1, device_id=peer, device_id_type=MESH)
    count += len(early.to) + len(early.frm)
    fetch = pltpu.make_async_copy(p_hbm, p_ref, psem)
    fetch.start()
    load = pltpu.make_async_copy(a_ref, av, asem)
    load.start()
    outs = []

    def put(src, dst):
        copy = pltpu.make_async_copy(src, dst, osem.at[len(outs)])
        copy.start()
        outs.append(copy)

    fetch.wait()
    p = p_ref[...]
    src1[0:n, :] = mm(p, p, TN)
    src1[n:, :] = p[0:n, :] * jnp.where(row == 0, 1.0, 0.0)
    pl.semaphore_wait(sem, count)

    red = Reduce(out1, red1[0], red1[1], red1[2:], ncol)
    gc = red.gc
    red.start_x(src1)
    early.start_one()
    red.start_z()
    red.start_c()
    for j in range(4):
        early.forward(j)
    red.finish()

    def part(d):
        return pl.ds(pl.multiple_of(((c + d) % ncol) * sl, 8), sl)

    def wsend(d):
        return pltpu.make_async_remote_copy(
            src_ref=av.at[d * sl:(d + 1) * sl, 0:n], dst_ref=wbuf, send_sem=ws.at[d], recv_sem=wr,
            device_id=gc[d], device_id_type=MESH)

    def share(lanes, ssems, rsems):
        own = yw.at[part(0), lanes]
        return [send(own, own, ssems.at[d], rsems.at[d], gc[d]) for d in range(1, ncol)]

    def shared(lanes, ssems, rsems):
        for d in range(1, ncol):
            theirs = yw.at[part(ncol - d), lanes]
            pltpu.make_async_remote_copy(
                src_ref=theirs, dst_ref=theirs, send_sem=ssems.at[d], recv_sem=rsems.at[d],
                device_id=gc[d], device_id_type=MESH).wait_recv()

    load.wait()

    @pl.when(c == 0)
    def _():
        for d in range(1, ncol):
            wsend(d).start()
        wbuf[...] = av[0:sl, 0:n]

    with_identity(work, out1[0:n, :])
    chol_inv(work, rows)
    l1, l1i = factors(rows)

    xr = mm(p_ref[...], l1i, NT)
    src2[...] = mm(xr, xr, TN)
    red = Reduce(out2, red2[0], red2[1], red2[2:], ncol)
    red.start_x(src2)
    l1_ref[...] = l1
    put(l1_ref, l1_out)
    lead_ref[:, 0:n] = xr
    xt = mm(out1[n:, :], l1i, NT)

    @pl.when(c != 0)
    def _():
        wsend(1).wait_recv()

    yw[part(0), n:] = wbuf[...]
    wsends = share(slice(n, 2 * n), vs, vr_sem)
    red.start_z()

    def block(k):
        early.block(k)
        xk = mm(pc[k], l1i, NT)
        vc_ref[k] = xk
        return mm3(halves(av[:, k * height:(k + 1) * height]), halves(xk))

    acc = block(0)
    acc = acc + block(1)
    acc = acc + block(2)
    red.start_c()
    acc = acc + block(3)
    yp[...] = acc
    early.finish()
    ybuf[0] = yp[part(0), :]
    ysends = [send(yp.at[part(d), :], ybuf.at[d], ys.at[d], yr.at[d], gc[d]) for d in range(1, ncol)]
    red.finish()
    fsends = []

    def spread():
        for copy in ysends:
            copy.wait_recv()
        yw[part(0), 0:n] = slot_sum(ybuf, c, ncol)
        fsends.extend(share(slice(0, n), fs, fr))

    with_identity(work, out2[...])
    chol_inv(work, rows, {3: spread})
    l2, l2i = factors(rows)
    shared(slice(n, 2 * n), vs, vr_sem)
    shared(slice(0, n), fs, fr)

    avr[...] = mm(yw[:, 0:n], l2i, NT) + yw[:, n:]
    late.start_one()
    vr = mm(lead_ref[:, 0:n], l2i, NT) + jnp.where(eyes((height, n), row * height), 1.0, 0.0)
    src3[...] = mm(vr, avr[...], TN)
    red = Reduce(out3, red3[0], red3[1], red3[2:], ncol)
    red.start_x(src3)
    with_identity(work, mm(xt, l2i, NT).T + jnp.where(eyes((n, n)), 1.0, 0.0))
    near = (1, 3)
    gj_inverse(work, {4: red.start_z, 6: lambda: late.forward(0, near)})
    k = work[:, n:]
    for j in range(1, 4):
        late.forward(j, near)
    red.start_c()
    for j in range(4):
        shift = (c * 4 + j) * height
        vc_ref[j] = mm(vc_ref[j], l2i, NT) + jnp.where(eyes((height, n), shift), 1.0, 0.0)
        put(vc_ref.at[j], vc_out.at[j])
    band_ref[...] = -mm(l2, l1_ref[...], (((0,), (1,)), ((), ())))
    put(band_ref, band_out)
    late.relay(0)
    late.relay(1)
    red.finish()
    inner = mm(k, mm(out3[...], k), TN)
    right = jnp.concatenate([
        jnp.concatenate([jnp.zeros((n, n), F32), k], axis=1),
        jnp.concatenate([k.T, -0.5 * (inner + inner.T)], axis=1)], axis=0)
    lead_ref[...] = mm(jnp.concatenate([avr[...], vr], axis=1), right)
    put(lead_ref, lead_out)
    late.relay(2)
    late.relay(3)
    for j in range(4):
        at = late.nearest(j)
        late.relayed(at)
        put(avc_ref.at[at], avc_out.at[at])
    late.finish()
    for copy in outs:
        copy.wait()
    for copy in ysends + fsends + wsends:
        copy.wait_send()

    @pl.when(c == 0)
    def _():
        for d in range(1, ncol):
            wsend(d).wait_send()


def last_kernel(l1_in, band_in, lead_in, avc_in, vc_in, a_ref, out_ref, band_ref, l1_ref,
                lead_ref, pairs, abuf, obuf, leadsem, insem, outsem):
    parts, height, n = avc_in.shape
    width = height // 2
    first = pltpu.make_async_copy(lead_in, lead_ref, leadsem)
    first.start()
    loads = []
    for k in range(parts):
        loads.append([
            pltpu.make_async_copy(avc_in.at[k], pairs.at[k, :, 0:n], insem.at[k, 0]),
            pltpu.make_async_copy(vc_in.at[k], pairs.at[k, :, n:2 * n], insem.at[k, 1]),
            pltpu.make_async_copy(a_ref.at[:, k * height:(k + 1) * height], abuf.at[k], insem.at[k, 2])])
        for copy in loads[k]:
            copy.start()
    band_ref[...] = band_in[...]
    l1_ref[...] = l1_in[...]
    first.wait()
    lead = halves(lead_ref[...])
    stores = []
    for k in range(parts):
        loads[k][0].wait()
        loads[k][1].wait()
        for h in range(2):
            cols = slice(h * width, (h + 1) * width)
            prod = mm3(lead, halves(pairs[k, cols, :]), NT)
            if h == 0:
                loads[k][2].wait()
            obuf[k, :, cols] = abuf[k, :, cols] - prod
            at = k * height + h * width
            copy = pltpu.make_async_copy(obuf.at[k, :, cols], out_ref.at[:, at:at + width], outsem.at[k, h])
            copy.start()
            stores.append(copy)
    for copy in stores:
        copy.wait()


def body(ncol, panel, trailing):
    n = panel.shape[1]
    height, width = trailing.shape
    sl = height // ncol
    dma = pltpu.SemaphoreType.DMA

    def vmem(*shape):
        return pltpu.VMEM(shape, F32)

    l1, band, lead, avc, vc = pl.pallas_call(
        functools.partial(main_kernel, ncol),
        out_shape=(struct(n, n), struct(n, n), struct(height, 2 * n), struct(4, height, n), struct(4, height, n)),
        in_specs=[ANY, ANY], out_specs=(ANY,) * 5,
        scratch_shapes=[vmem(2 * n, n), vmem(2 * n, n), vmem(n, n), vmem(n, n), vmem(n, n), vmem(n, n)]
        + reduce_scratch(2 * n, ncol) + reduce_scratch(n, ncol) + reduce_scratch(n, ncol)
        + gather_sems() + gather_sems()
        + [vmem(height, width), vmem(4, height, n), vmem(n, 2 * n), vmem(n, 2 * n), vmem(height, n),
           vmem(ncol, sl, n), vmem(sl, n), vmem(height, 2 * n), vmem(height, n),
           vmem(height, n), vmem(n, n), vmem(n, n), vmem(height, 2 * n), vmem(4, height, n), vmem(4, height, n)]
        + [dma, dma, dma((16,)), dma((ncol,)), dma((ncol,)), dma((ncol,)), dma]
        + [dma((ncol,)), dma((ncol,)), dma((ncol,)), dma((ncol,))],
        compiler_params=pltpu.CompilerParams(collective_id=0, has_side_effects=True, vmem_limit_bytes=60 << 20),
        name="main")(panel, trailing)
    reduced, band, l1 = pl.pallas_call(
        last_kernel, out_shape=(struct(height, width), struct(n, n), struct(n, n)),
        in_specs=[VM] * 2 + [ANY] * 4, out_specs=(ANY, VM, VM),
        scratch_shapes=[vmem(height, 2 * n), vmem(4, height, 2 * n), vmem(4, height, width // 4), vmem(4, height, width // 4),
                        dma, dma((4, 3)), dma((4, 2))],
        compiler_params=pltpu.CompilerParams(vmem_limit_bytes=60 << 20), name="last",
    )(l1, band, lead, avc, vc, trailing)
    return reduced, band, l1


def solution(mesh):
    return jax.shard_map(
        functools.partial(body, mesh.shape["col"]), mesh=mesh, in_specs=(P("row", None), P("row", "col")),
        out_specs=(P("row", "col"), P(), P()), check_vma=False)
```

```python
import functools

import jax
import jax.numpy as jnp
from jax import lax
from jax.experimental import pallas as pl
from jax.experimental.pallas import tpu as pltpu
from jax.sharding import PartitionSpec as P

HIGH = lax.Precision.HIGHEST
F32 = jnp.float32
BF16 = jnp.bfloat16
MESH = pl.DeviceIdType.MESH
NX, NZ = 4, 8
BS = 16
NN = (((1,), (0,)), ((), ()))
NT = (((1,), (1,)), ((), ()))
TN = (((0,), (0,)), ((), ()))


def mm(a, b, dims=NN):
    return lax.dot_general(a, b, dims, precision=HIGH, preferred_element_type=F32)


def halves(a):
    top = a.astype(BF16)
    return top, (a - top.astype(F32)).astype(BF16)


def mm3(a, b, dims=NN):
    def one(p, q):
        return lax.dot_general(p, q, dims, preferred_element_type=F32)
    return one(a[0], b[0]) + (one(a[0], b[1]) + one(a[1], b[0]))


def eyes(shape, shift=0):
    return (lax.broadcasted_iota(jnp.int32, shape, 0) + shift) == lax.broadcasted_iota(jnp.int32, shape, 1)


def over(row, count):
    return jnp.broadcast_to(row, (count, row.shape[1]))


def eliminate(work, lo, hot, jordan):
    n = work.shape[0]
    bs = len(hot)
    rows = work[lo:lo + bs, :]
    col = [jnp.broadcast_to(rows[:, lo + k:lo + k + 1], (bs, n)) for k in range(bs)]
    pivots = []
    left, right = rows[:, 0:n], rows[:, n:]
    for t in range(bs):
        pivot = over(col[t][t:t + 1, :], bs)
        pivots.append(pivot[0:1, :])
        inv = 1.0 / pivot
        f = col[t] - hot[t] if jordan else jnp.where(hot[t], col[t], 0.0)
        for k in range(t + 1, bs):
            col[k] = col[k] - (f * over(col[k][t:t + 1, :], bs)) * inv
        g = f * inv
        left = left - g * over(left[t:t + 1, :], bs)
        right = right - g * over(right[t:t + 1, :], bs)
    return left, right, pivots


def chol_inv(work, rows, hooks=()):
    n = work.shape[0]
    at = lax.broadcasted_iota(jnp.int32, (BS, n), 0)
    hot = [at > t for t in range(BS)]
    for b in range(n // BS):
        lo = b * BS
        left, right, pivots = eliminate(work, lo, hot, False)
        scale = lax.rsqrt(jnp.concatenate(pivots, axis=0))
        blk = jnp.concatenate([left * scale, right * scale], axis=1)
        rows[lo:lo + BS, :] = blk
        if lo + BS < n:
            work[lo + BS:, :] = work[lo + BS:, :] - mm(blk[:, lo + BS:n], blk, TN)
        if b in hooks:
            hooks[b]()


def gj_inverse(work, hooks=()):
    n = work.shape[0]
    at = lax.broadcasted_iota(jnp.int32, (BS, n), 0)
    hot = [jnp.where(at == t, 1.0, 0.0) for t in range(BS)]
    for b in range(n // BS):
        lo = b * BS
        left, right, _ = eliminate(work, lo, hot, True)
        both = jnp.concatenate([left, right], axis=1)
        cols = work[:, lo:lo + BS]
        rowi = lax.broadcasted_iota(jnp.int32, cols.shape, 0)
        cols = jnp.where((rowi >= lo) & (rowi < lo + BS), 0.0, cols)
        work[...] = work[...] - mm(cols, both)
        work[lo:lo + BS, :] = both
        if b in hooks:
            hooks[b]()


def with_identity(work, square):
    n = work.shape[0]
    work[:, 0:n] = square
    work[:, n:] = jnp.where(eyes((n, n)), 1.0, 0.0)


def factors(rows):
    n = rows.shape[0]
    low = lax.broadcasted_iota(jnp.int32, (n, n), 0) >= lax.broadcasted_iota(jnp.int32, (n, n), 1)
    return jnp.where(low, rows[:, 0:n].T, 0.0), jnp.where(low, rows[:, n:], 0.0)


def place():
    row = lax.axis_index("row")
    return row // NZ, row % NZ, lax.axis_index("col")


def groups(ncol):
    x, z, c = place()
    gx = [(((x + d) % NX) * NZ + z, c) for d in range(NX)]
    gz = [(x * NZ + (z + d) % NZ, c) for d in range(NZ)]
    gc = [(x * NZ + z, (c + d) % ncol) for d in range(ncol)]
    return gx, gz, gc


def greet(ncol):
    sem = pltpu.get_barrier_semaphore()
    gx, gz, gc = groups(ncol)
    peers = gx[1:] + gz[1:] + gc[1:]
    for peer in peers:
        pl.semaphore_signal(sem, inc=1, device_id=peer, device_id_type=MESH)
    return sem, len(peers)


def send(src, dst, ss, rs, peer):
    copy = pltpu.make_async_remote_copy(
        src_ref=src, dst_ref=dst, send_sem=ss, recv_sem=rs, device_id=peer, device_id_type=MESH)
    copy.start()
    return copy


def slot_sum(buf, me, count):
    total = buf[me]
    for a in range(1, count):
        total = total + buf[(me + count - a) % count]
    return total


def all_in(view, sem, peer):
    pltpu.make_async_remote_copy(
        src_ref=view, dst_ref=view, send_sem=sem, recv_sem=sem, device_id=peer, device_id_type=MESH).wait_recv()


def all_out(view, sem, peer):
    pltpu.make_async_remote_copy(
        src_ref=view, dst_ref=view, send_sem=sem, recv_sem=sem, device_id=peer, device_id_type=MESH).wait_send()


class Reduce:
    def __init__(self, out, xbuf, zbuf, sems, ncol):
        self.out, self.xbuf, self.zbuf, self.ncol = out, xbuf, zbuf, ncol
        self.xs, self.xr, self.zs, self.zr, self.cs, self.cr = sems
        self.gx, self.gz, self.gc = groups(ncol)
        self.x, self.z, self.c = place()
        self.sl = out.shape[0] // ncol

    def part(self):
        return pl.ds(pl.multiple_of(self.c * self.sl, 8), self.sl)

    def start_x(self, src):
        self.xbuf[0] = src[self.part(), :]
        for d in range(1, NX):
            send(self.xbuf.at[0], self.xbuf.at[d], self.xs, self.xr, self.gx[d])

    def start_z(self):
        all_in(self.xbuf.at[1:NX], self.xr, self.gx[1])
        self.zbuf[0] = slot_sum(self.xbuf, self.x, NX)
        for d in range(1, NZ):
            send(self.zbuf.at[0], self.zbuf.at[d], self.zs, self.zr, self.gz[d])

    def start_c(self):
        all_in(self.zbuf.at[1:NZ], self.zr, self.gz[1])
        self.out[self.part(), :] = slot_sum(self.zbuf, self.z, NZ)
        mine = self.out.at[self.part(), :]
        for d in range(1, self.ncol):
            send(mine, mine, self.cs, self.cr, self.gc[d])

    def finish(self):
        rest = self.out.at[0:(self.ncol - 1) * self.sl, :]
        all_in(rest, self.cr, self.gc[1])
        all_out(self.xbuf.at[1:NX], self.xs, self.gx[1])
        all_out(self.zbuf.at[1:NZ], self.zs, self.gz[1])
        all_out(rest, self.cs, self.gc[1])


def reduce_scratch(height, ncol):
    sl = height // ncol
    dma = pltpu.SemaphoreType.DMA
    return [pltpu.VMEM((NX, sl, 128), F32), pltpu.VMEM((NZ, sl, 128), F32),
            dma, dma, dma, dma, dma, dma]


VM = pl.BlockSpec(memory_space=pltpu.VMEM)
ANY = pl.BlockSpec(memory_space=pl.ANY)


def comm_params(cid):
    return pltpu.CompilerParams(collective_id=cid, has_side_effects=True, vmem_limit_bytes=60 << 20)


def turn(y):
    return (y + 2) % 3 + y // 3


def unturn(t):
    return (t + 1) % 3 * (1 - t // 3) + 3 * (t // 3)


class Gather:
    def __init__(self, src, out, sems, ncol):
        self.src, self.out = src, out
        self.s1, self.r1, self.s2, self.r2, self.s3, self.r3 = sems
        self.x, self.z, self.c = place()
        y, core = self.c // 2, self.c % 2
        self.quarter = src.shape[0] // NX
        xd = (turn(y) + NX - self.x) % NX
        self.xd = xd
        self.to = [((xd * NZ) + 2 * j + core, self.x * 2 + self.z // 4) for j in range(4)]
        ys = unturn((self.x + y) % NX)
        self.frm = [(y * NZ + 4 * core + k, ys * 2 + self.z % 2) for k in range(4)]
        self.gx = groups(ncol)[0]

    def rows(self, x):
        return pl.ds(pl.multiple_of(x * self.quarter, 128), self.quarter)

    def start_one(self):
        k = self.z % 4
        for j in range(4):
            send(self.src.at[self.rows(self.xd), :], self.out.at[k, self.rows(self.xd), :],
                 self.s1, self.r1.at[k], self.to[j])

    def nearest(self, j):
        return (self.z + j) % 4

    def forward(self, j, steps=(1, 2, 3)):
        k = self.nearest(j)
        part = self.out.at[k, self.rows(self.x), :]
        all_in(part, self.r1.at[k], self.frm[0])
        for d in steps:
            send(part, part, self.s2, self.r2.at[k], self.gx[d])

    def relay(self, j):
        k = self.nearest(j)
        half = self.quarter // 2
        all_in(self.out.at[k, 0:2 * self.quarter, :], self.r2.at[k], self.gx[1])
        for i, d in enumerate((1, 3)):
            x = (self.x + NX - d) % NX
            part = self.out.at[k, pl.ds(pl.multiple_of(x * self.quarter + i * half, 8), half), :]
            send(part, part, self.s3, self.r3.at[k], self.gx[d])

    def block(self, k):
        all_in(self.out.at[k, 0:3 * self.quarter, :], self.r2.at[k], self.gx[1])

    def relayed(self, k):
        all_in(self.out.at[k, 0:self.quarter, :], self.r3.at[k], self.gx[1])

    def finish(self, near):
        all_out(self.out.at[:, 0:self.quarter, :], self.s1, self.to[0])
        all_out(self.out.at[:, 0:near * self.quarter, :], self.s2, self.gx[1])
        if near == 2:
            all_out(self.out.at[:, 0:self.quarter, :], self.s3, self.gx[1])


def gather_sems():
    dma = pltpu.SemaphoreType.DMA
    return [dma, dma((4,)), dma, dma((4,)), dma, dma((4,))]


VM = pl.BlockSpec(memory_space=pltpu.VMEM)
ANY = pl.BlockSpec(memory_space=pl.ANY)


def struct(*shape):
    return jax.ShapeDtypeStruct(shape, F32)


def main_kernel(ncol, p_hbm, a_ref, l1_out, band_out, lead_out, avc_out, vc_out, *scratch):
    scratch = list(scratch)

    def take(count):
        head = scratch[:count]
        del scratch[:count]
        return head

    src1, out1, src2, out2, src3, out3 = take(6)
    red1, red2, red3 = take(8), take(8), take(8)
    gs1, gs2 = take(6), take(6)
    av, pc, work, rows, yp, ybuf, wbuf, yw, avr = take(9)
    p_ref, l1_ref, band_ref, lead_ref, avc_ref, vc_ref = take(6)
    asem, psem, osem, ys, yr, ws, wr, vs, vr_sem, fs, fr = take(11)
    n = p_ref.shape[1]
    height = p_ref.shape[0]
    sl = height // ncol
    row, c = lax.axis_index("row"), lax.axis_index("col")

    sem, count = greet(ncol)
    early = Gather(p_ref, pc, gs1, ncol)
    late = Gather(avr, avc_ref, gs2, ncol)
    for peer in early.to + early.frm:
        pl.semaphore_signal(sem, inc=1, device_id=peer, device_id_type=MESH)
    count += len(early.to) + len(early.frm)
    fetch = pltpu.make_async_copy(p_hbm, p_ref, psem)
    fetch.start()
    load = pltpu.make_async_copy(a_ref, av, asem)
    load.start()
    outs = []

    def put(src, dst):
        copy = pltpu.make_async_copy(src, dst, osem.at[len(outs)])
        copy.start()
        outs.append(copy)

    fetch.wait()
    p = p_ref[...]
    src1[0:n, :] = mm(p, p, TN)
    src1[n:, :] = p[0:n, :] * jnp.where(row == 0, 1.0, 0.0)
    pl.semaphore_wait(sem, count)

    red = Reduce(out1, red1[0], red1[1], red1[2:], ncol)
    gc = red.gc
    red.start_x(src1)
    red.start_z()
    early.start_one()
    red.start_c()
    red.finish()
    for j in range(4):
        early.forward(j)

    def part(d):
        return pl.ds(pl.multiple_of(((c + d) % ncol) * sl, 8), sl)

    def wsend(d):
        return pltpu.make_async_remote_copy(
            src_ref=av.at[d * sl:(d + 1) * sl, 0:n], dst_ref=wbuf, send_sem=ws, recv_sem=wr,
            device_id=gc[d], device_id_type=MESH)

    def share(lanes, ssem, rsem):
        own = yw.at[part(0), lanes]
        for d in range(1, ncol):
            send(own, own, ssem, rsem, gc[d])

    def rest(lanes):
        return yw.at[0:(ncol - 1) * sl, lanes]

    load.wait()

    @pl.when(c == 0)
    def _():
        for d in range(1, ncol):
            wsend(d).start()
        wbuf[...] = av[0:sl, 0:n]

    with_identity(work, out1[0:n, :])
    chol_inv(work, rows)
    l1, l1i = factors(rows)

    xr = mm(p_ref[...], l1i, NT)
    src2[...] = mm(xr, xr, TN)
    red = Reduce(out2, red2[0], red2[1], red2[2:], ncol)
    red.start_x(src2)
    l1_ref[...] = l1
    put(l1_ref, l1_out)
    lead_ref[:, 0:n] = xr
    xt = mm(out1[n:, :], l1i, NT)

    @pl.when(c != 0)
    def _():
        wsend(1).wait_recv()

    yw[part(0), n:] = wbuf[...]
    share(slice(n, 2 * n), vs, vr_sem)
    red.start_z()

    def block(k):
        early.block(k)
        xk = mm(pc[k], l1i, NT)
        vc_ref[k] = xk
        return mm3(halves(av[:, k * height:(k + 1) * height]), halves(xk))

    acc = block(0)
    acc = acc + block(1)
    acc = acc + block(2)
    red.start_c()
    acc = acc + block(3)
    yp[...] = acc
    early.finish(3)
    ybuf[0] = yp[part(0), :]
    for d in range(1, ncol):
        send(yp.at[part(d), :], ybuf.at[d], ys, yr, gc[d])
    red.finish()

    def spread():
        all_in(ybuf.at[1:ncol], yr, gc[1])
        yw[part(0), 0:n] = slot_sum(ybuf, c, ncol)
        share(slice(0, n), fs, fr)

    with_identity(work, out2[...])
    chol_inv(work, rows, {1: spread})
    l2, l2i = factors(rows)
    vr = mm(lead_ref[:, 0:n], l2i, NT) + jnp.where(eyes((height, n), row * height), 1.0, 0.0)
    with_identity(work, mm(xt, l2i, NT).T + jnp.where(eyes((n, n)), 1.0, 0.0))
    for j in range(4):
        shift = (c * 4 + j) * height
        vc_ref[j] = mm(vc_ref[j], l2i, NT) + jnp.where(eyes((height, n), shift), 1.0, 0.0)
        put(vc_ref.at[j], vc_out.at[j])
    all_in(rest(slice(n, 2 * n)), vr_sem, gc[1])
    all_in(rest(slice(0, n)), fr, gc[1])

    avr[...] = mm(yw[:, 0:n], l2i, NT) + yw[:, n:]
    late.start_one()
    src3[...] = mm(vr, avr[...], TN)
    red = Reduce(out3, red3[0], red3[1], red3[2:], ncol)
    red.start_x(src3)
    near = (1, 3)
    gj_inverse(work, {4: red.start_z, 6: lambda: late.forward(0, near)})
    k = work[:, n:]
    for j in range(1, 4):
        late.forward(j, near)
    red.start_c()
    late.relay(0)
    late.relay(1)
    band_ref[...] = -mm(l2, l1_ref[...], (((0,), (1,)), ((), ())))
    put(band_ref, band_out)
    late.relay(2)
    late.relay(3)
    red.finish()
    inner = mm(k, mm(out3[...], k), TN)
    right = jnp.concatenate([
        jnp.concatenate([jnp.zeros((n, n), F32), k], axis=1),
        jnp.concatenate([k.T, -0.5 * (inner + inner.T)], axis=1)], axis=0)
    lead_ref[...] = mm(jnp.concatenate([avr[...], vr], axis=1), right)
    put(lead_ref, lead_out)
    for j in range(4):
        at = late.nearest(j)
        late.relayed(at)
        put(avc_ref.at[at], avc_out.at[at])
    late.finish(2)
    for copy in outs:
        copy.wait()
    all_out(ybuf.at[1:ncol], ys, gc[1])
    all_out(rest(slice(0, n)), fs, gc[1])
    all_out(rest(slice(n, 2 * n)), vs, gc[1])

    @pl.when(c == 0)
    def _():
        all_out(rest(slice(0, n)), ws, gc[1])


def last_kernel(l1_in, band_in, lead_ref, avc_ref, vc_ref, a_ref, out_ref, band_ref, l1_ref, abuf, obuf, insem, outsem):
    width = avc_ref.shape[1]
    loads = [pltpu.make_async_copy(a_ref.at[:, k * width:(k + 1) * width], abuf.at[k], insem.at[k]) for k in range(4)]
    for copy in loads:
        copy.start()
    band_ref[...] = band_in[...]
    l1_ref[...] = l1_in[...]
    lead = halves(lead_ref[...])
    stores = []
    for k in range(4):
        tail = halves(jnp.concatenate([avc_ref[k], vc_ref[k]], axis=1))
        prod = mm3(lead, tail, NT)
        loads[k].wait()
        obuf[k] = abuf[k] - prod
        copy = pltpu.make_async_copy(obuf.at[k], out_ref.at[:, k * width:(k + 1) * width], outsem.at[k])
        copy.start()
        stores.append(copy)
    for copy in stores:
        copy.wait()


def body(ncol, panel, trailing):
    n = panel.shape[1]
    height, width = trailing.shape
    sl = height // ncol
    dma = pltpu.SemaphoreType.DMA

    def vmem(*shape):
        return pltpu.VMEM(shape, F32)

    l1, band, lead, avc, vc = pl.pallas_call(
        functools.partial(main_kernel, ncol),
        out_shape=(struct(n, n), struct(n, n), struct(height, 2 * n), struct(4, height, n), struct(4, height, n)),
        in_specs=[ANY, ANY], out_specs=(ANY,) * 5,
        scratch_shapes=[vmem(2 * n, n), vmem(2 * n, n), vmem(n, n), vmem(n, n), vmem(n, n), vmem(n, n)]
        + reduce_scratch(2 * n, ncol) + reduce_scratch(n, ncol) + reduce_scratch(n, ncol)
        + gather_sems() + gather_sems()
        + [vmem(height, width), vmem(4, height, n), vmem(n, 2 * n), vmem(n, 2 * n), vmem(height, n),
           vmem(ncol, sl, n), vmem(sl, n), vmem(height, 2 * n), vmem(height, n),
           vmem(height, n), vmem(n, n), vmem(n, n), vmem(height, 2 * n), vmem(4, height, n), vmem(4, height, n)]
        + [dma, dma, dma((11,)), dma, dma, dma, dma, dma, dma, dma, dma],
        compiler_params=pltpu.CompilerParams(collective_id=0, has_side_effects=True, vmem_limit_bytes=60 << 20),
        name="main")(panel, trailing)
    reduced, band, l1 = pl.pallas_call(
        last_kernel, out_shape=(struct(height, width), struct(n, n), struct(n, n)),
        in_specs=[VM] * 5 + [ANY], out_specs=(ANY, VM, VM),
        scratch_shapes=[vmem(4, height, width // 4), vmem(4, height, width // 4), dma((4,)), dma((4,))],
        compiler_params=pltpu.CompilerParams(vmem_limit_bytes=60 << 20), name="last",
    )(l1, band, lead, avc, vc, trailing)
    return reduced, band, l1


def solution(mesh):
    return jax.shard_map(
        functools.partial(body, mesh.shape["col"]), mesh=mesh, in_specs=(P("row", None), P("row", "col")),
        out_specs=(P("row", "col"), P(), P()), check_vma=False)
```

```python
import functools

import jax
import jax.numpy as jnp
from jax import lax
from jax.experimental import pallas as pl
from jax.experimental.pallas import tpu as pltpu
from jax.sharding import PartitionSpec as P

HIGH = lax.Precision.HIGHEST
F32 = jnp.float32
BF16 = jnp.bfloat16
MESH = pl.DeviceIdType.MESH
NX, NZ = 4, 8
BS = 16
NN = (((1,), (0,)), ((), ()))
NT = (((1,), (1,)), ((), ()))
TN = (((0,), (0,)), ((), ()))


def mm(a, b, dims=NN):
    return lax.dot_general(a, b, dims, precision=HIGH, preferred_element_type=F32)


def halves(a):
    top = a.astype(BF16)
    return top, (a - top.astype(F32)).astype(BF16)


def mm3(a, b, dims=NN):
    def one(p, q):
        return lax.dot_general(p, q, dims, preferred_element_type=F32)
    return one(a[0], b[0]) + (one(a[0], b[1]) + one(a[1], b[0]))


def eyes(shape, shift=0):
    return (lax.broadcasted_iota(jnp.int32, shape, 0) + shift) == lax.broadcasted_iota(jnp.int32, shape, 1)


def over(row, count):
    return jnp.broadcast_to(row, (count, row.shape[1]))


def eliminate(work, lo, hot, jordan):
    n = work.shape[0]
    bs = len(hot)
    rows = work[lo:lo + bs, :]
    col = [jnp.broadcast_to(rows[:, lo + k:lo + k + 1], (bs, n)) for k in range(bs)]
    pivots = []
    left, right = rows[:, 0:n], rows[:, n:]
    for t in range(bs):
        pivot = over(col[t][t:t + 1, :], bs)
        pivots.append(pivot[0:1, :])
        inv = 1.0 / pivot
        f = col[t] - hot[t] if jordan else jnp.where(hot[t], col[t], 0.0)
        for k in range(t + 1, bs):
            col[k] = col[k] - (f * over(col[k][t:t + 1, :], bs)) * inv
        g = f * inv
        left = left - g * over(left[t:t + 1, :], bs)
        right = right - g * over(right[t:t + 1, :], bs)
    return left, right, pivots


def chol_inv(work, rows, hooks=()):
    n = work.shape[0]
    at = lax.broadcasted_iota(jnp.int32, (BS, n), 0)
    hot = [at > t for t in range(BS)]
    for b in range(n // BS):
        lo = b * BS
        left, right, pivots = eliminate(work, lo, hot, False)
        scale = lax.rsqrt(jnp.concatenate(pivots, axis=0))
        blk = jnp.concatenate([left * scale, right * scale], axis=1)
        rows[lo:lo + BS, :] = blk
        if lo + BS < n:
            work[lo + BS:, :] = work[lo + BS:, :] - mm(blk[:, lo + BS:n], blk, TN)
        if b in hooks:
            hooks[b]()


def gj_inverse(work, hooks=()):
    n = work.shape[0]
    at = lax.broadcasted_iota(jnp.int32, (BS, n), 0)
    hot = [jnp.where(at == t, 1.0, 0.0) for t in range(BS)]
    for b in range(n // BS):
        lo = b * BS
        left, right, _ = eliminate(work, lo, hot, True)
        both = jnp.concatenate([left, right], axis=1)
        cols = work[:, lo:lo + BS]
        rowi = lax.broadcasted_iota(jnp.int32, cols.shape, 0)
        cols = jnp.where((rowi >= lo) & (rowi < lo + BS), 0.0, cols)
        work[...] = work[...] - mm(cols, both)
        work[lo:lo + BS, :] = both
        if b in hooks:
            hooks[b]()


def with_identity(work, square):
    n = work.shape[0]
    work[:, 0:n] = square
    work[:, n:] = jnp.where(eyes((n, n)), 1.0, 0.0)


def factors(rows):
    n = rows.shape[0]
    low = lax.broadcasted_iota(jnp.int32, (n, n), 0) >= lax.broadcasted_iota(jnp.int32, (n, n), 1)
    return jnp.where(low, rows[:, 0:n].T, 0.0), jnp.where(low, rows[:, n:], 0.0)


def place():
    row = lax.axis_index("row")
    return row // NZ, row % NZ, lax.axis_index("col")


def groups(ncol):
    x, z, c = place()
    gx = [(((x + d) % NX) * NZ + z, c) for d in range(NX)]
    gz = [(x * NZ + (z + d) % NZ, c) for d in range(NZ)]
    gc = [(x * NZ + z, (c + d) % ncol) for d in range(ncol)]
    return gx, gz, gc


def greet(ncol):
    sem = pltpu.get_barrier_semaphore()
    gx, gz, gc = groups(ncol)
    peers = gx[1:] + gz[1:] + gc[1:]
    for peer in peers:
        pl.semaphore_signal(sem, inc=1, device_id=peer, device_id_type=MESH)
    return sem, len(peers)


def send(src, dst, ss, rs, peer):
    copy = pltpu.make_async_remote_copy(
        src_ref=src, dst_ref=dst, send_sem=ss, recv_sem=rs, device_id=peer, device_id_type=MESH)
    copy.start()
    return copy


def slot_sum(buf, me, count):
    total = buf[me]
    for a in range(1, count):
        total = total + buf[(me + count - a) % count]
    return total


def all_in(view, sem, peer):
    pltpu.make_async_remote_copy(
        src_ref=view, dst_ref=view, send_sem=sem, recv_sem=sem, device_id=peer, device_id_type=MESH).wait_recv()


def all_out(view, sem, peer):
    pltpu.make_async_remote_copy(
        src_ref=view, dst_ref=view, send_sem=sem, recv_sem=sem, device_id=peer, device_id_type=MESH).wait_send()


class Reduce:
    def __init__(self, out, first, second, sems, ncol, z_first=False):
        self.out, self.first, self.second, self.ncol = out, first, second, ncol
        self.s1, self.r1, self.s2, self.r2, self.cs, self.cr = sems
        gx, gz, self.gc = groups(ncol)
        x, z, self.c = place()
        self.g1, self.g2 = (gz, gx) if z_first else (gx, gz)
        self.i1, self.i2 = (z, x) if z_first else (x, z)
        self.sl = out.shape[0] // ncol

    def part(self):
        return pl.ds(pl.multiple_of(self.c * self.sl, 8), self.sl)

    def start_first(self, src):
        self.first[0] = src[self.part(), :]
        for d in range(1, len(self.g1)):
            send(self.first.at[0], self.first.at[d], self.s1, self.r1, self.g1[d])

    def start_second(self):
        count = len(self.g1)
        all_in(self.first.at[1:count], self.r1, self.g1[1])
        self.second[0] = slot_sum(self.first, self.i1, count)
        for d in range(1, len(self.g2)):
            send(self.second.at[0], self.second.at[d], self.s2, self.r2, self.g2[d])

    def start_c(self):
        count = len(self.g2)
        all_in(self.second.at[1:count], self.r2, self.g2[1])
        self.out[self.part(), :] = slot_sum(self.second, self.i2, count)
        mine = self.out.at[self.part(), :]
        for d in range(1, self.ncol):
            send(mine, mine, self.cs, self.cr, self.gc[d])

    def finish(self):
        rest = self.out.at[0:(self.ncol - 1) * self.sl, :]
        all_in(rest, self.cr, self.gc[1])
        all_out(self.first.at[1:len(self.g1)], self.s1, self.g1[1])
        all_out(self.second.at[1:len(self.g2)], self.s2, self.g2[1])
        all_out(rest, self.cs, self.gc[1])


def reduce_scratch(height, ncol):
    sl = height // ncol
    dma = pltpu.SemaphoreType.DMA
    return [pltpu.VMEM((NX, sl, 128), F32), pltpu.VMEM((NZ, sl, 128), F32),
            dma, dma, dma, dma, dma, dma]


VM = pl.BlockSpec(memory_space=pltpu.VMEM)
ANY = pl.BlockSpec(memory_space=pl.ANY)


def comm_params(cid):
    return pltpu.CompilerParams(collective_id=cid, has_side_effects=True, vmem_limit_bytes=60 << 20)


def turn(y):
    return (y + 2) % 3 + y // 3


def unturn(t):
    return (t + 1) % 3 * (1 - t // 3) + 3 * (t // 3)


class Gather:
    def __init__(self, src, out, sems, ncol):
        self.src, self.out = src, out
        self.s1, self.r1, self.s2, self.r2, self.s3, self.r3 = sems
        self.x, self.z, self.c = place()
        y, core = self.c // 2, self.c % 2
        self.quarter = src.shape[0] // NX
        xd = (turn(y) + NX - self.x) % NX
        self.xd = xd
        self.to = [((xd * NZ) + 2 * j + core, self.x * 2 + self.z // 4) for j in range(4)]
        ys = unturn((self.x + y) % NX)
        self.frm = [(y * NZ + 4 * core + k, ys * 2 + self.z % 2) for k in range(4)]
        self.gx = groups(ncol)[0]

    def rows(self, x):
        return pl.ds(pl.multiple_of(x * self.quarter, 128), self.quarter)

    def start_one(self):
        k = self.z % 4
        for j in range(4):
            send(self.src.at[self.rows(self.xd), :], self.out.at[k, self.rows(self.xd), :],
                 self.s1, self.r1.at[k], self.to[j])

    def nearest(self, j):
        return (self.z + j) % 4

    def forward(self, j, steps=(1, 2, 3)):
        k = self.nearest(j)
        part = self.out.at[k, self.rows(self.x), :]
        all_in(part, self.r1.at[k], self.frm[0])
        for d in steps:
            send(part, part, self.s2, self.r2.at[k], self.gx[d])

    def relay(self, j):
        k = self.nearest(j)
        half = self.quarter // 2
        all_in(self.out.at[k, 0:2 * self.quarter, :], self.r2.at[k], self.gx[1])
        for i, d in enumerate((1, 3)):
            x = (self.x + NX - d) % NX
            part = self.out.at[k, pl.ds(pl.multiple_of(x * self.quarter + i * half, 8), half), :]
            send(part, part, self.s3, self.r3.at[k], self.gx[d])

    def block(self, k):
        all_in(self.out.at[k, 0:3 * self.quarter, :], self.r2.at[k], self.gx[1])

    def relayed(self, k):
        all_in(self.out.at[k, 0:self.quarter, :], self.r3.at[k], self.gx[1])

    def finish(self, near):
        all_out(self.out.at[:, 0:self.quarter, :], self.s1, self.to[0])
        all_out(self.out.at[:, 0:near * self.quarter, :], self.s2, self.gx[1])
        if near == 2:
            all_out(self.out.at[:, 0:self.quarter, :], self.s3, self.gx[1])


def gather_sems():
    dma = pltpu.SemaphoreType.DMA
    return [dma, dma((4,)), dma, dma((4,)), dma, dma((4,))]


VM = pl.BlockSpec(memory_space=pltpu.VMEM)
ANY = pl.BlockSpec(memory_space=pl.ANY)


def struct(*shape):
    return jax.ShapeDtypeStruct(shape, F32)


def main_kernel(ncol, p_hbm, a_ref, l1_out, band_out, lead_out, avc_out, vc_out, *scratch):
    scratch = list(scratch)

    def take(count):
        head = scratch[:count]
        del scratch[:count]
        return head

    src1, out1, src2, out2, src3, out3 = take(6)
    red1, red2, red3 = take(8), take(8), take(8)
    gs1, gs2 = take(6), take(6)
    av, pc, work, rows, yp, ybuf, wbuf, yw, avr = take(9)
    p_ref, l1_ref, band_ref, lead_ref, avc_ref, vc_ref = take(6)
    asem, psem, osem, ys, yr, ws, wr, vs, vr_sem, fs, fr = take(11)
    n = p_ref.shape[1]
    height = p_ref.shape[0]
    sl = height // ncol
    row, c = lax.axis_index("row"), lax.axis_index("col")

    sem, count = greet(ncol)
    early = Gather(p_ref, pc, gs1, ncol)
    late = Gather(avr, avc_ref, gs2, ncol)
    for peer in early.to + early.frm:
        pl.semaphore_signal(sem, inc=1, device_id=peer, device_id_type=MESH)
    count += len(early.to) + len(early.frm)
    fetch = pltpu.make_async_copy(p_hbm, p_ref, psem)
    fetch.start()
    load = pltpu.make_async_copy(a_ref, av, asem)
    load.start()
    outs = []

    def put(src, dst):
        copy = pltpu.make_async_copy(src, dst, osem.at[len(outs)])
        copy.start()
        outs.append(copy)

    fetch.wait()
    p = p_ref[...]
    src1[0:n, :] = mm(p, p, TN)
    src1[n:, :] = p[0:n, :] * jnp.where(row == 0, 1.0, 0.0)
    pl.semaphore_wait(sem, count)

    red = Reduce(out1, red1[0], red1[1], red1[2:], ncol)
    gc = red.gc
    red.start_first(src1)
    red.start_second()
    early.start_one()
    red.start_c()
    for j in range(4):
        early.forward(j)
    red.finish()

    def part(d):
        return pl.ds(pl.multiple_of(((c + d) % ncol) * sl, 8), sl)

    def wsend(d):
        return pltpu.make_async_remote_copy(
            src_ref=av.at[d * sl:(d + 1) * sl, 0:n], dst_ref=wbuf, send_sem=ws, recv_sem=wr,
            device_id=gc[d], device_id_type=MESH)

    def share(lanes, ssem, rsem):
        own = yw.at[part(0), lanes]
        for d in range(1, ncol):
            send(own, own, ssem, rsem, gc[d])

    def rest(lanes):
        return yw.at[0:(ncol - 1) * sl, lanes]

    load.wait()

    @pl.when(c == 0)
    def _():
        for d in range(1, ncol):
            wsend(d).start()
        wbuf[...] = av[0:sl, 0:n]

    with_identity(work, out1[0:n, :])
    chol_inv(work, rows)
    l1, l1i = factors(rows)

    xr = mm(p_ref[...], l1i, NT)
    src2[...] = mm(xr, xr, TN)
    red = Reduce(out2, red2[1], red2[0], red2[2:], ncol, z_first=True)
    red.start_first(src2)
    l1_ref[...] = l1
    put(l1_ref, l1_out)
    lead_ref[:, 0:n] = xr
    xt = mm(out1[n:, :], l1i, NT)

    @pl.when(c != 0)
    def _():
        wsend(1).wait_recv()

    yw[part(0), n:] = wbuf[...]
    share(slice(n, 2 * n), vs, vr_sem)
    red.start_second()

    def block(k):
        early.block(k)
        xk = mm(pc[k], l1i, NT)
        vc_ref[k] = xk
        return mm3(halves(av[:, k * height:(k + 1) * height]), halves(xk))

    acc = block(0)
    acc = acc + block(1)
    acc = acc + block(2)
    red.start_c()
    acc = acc + block(3)
    yp[...] = acc
    early.finish(3)
    ybuf[0] = yp[part(0), :]
    for d in range(1, ncol):
        send(yp.at[part(d), :], ybuf.at[d], ys, yr, gc[d])
    red.finish()

    def spread():
        all_in(ybuf.at[1:ncol], yr, gc[1])
        yw[part(0), 0:n] = slot_sum(ybuf, c, ncol)
        share(slice(0, n), fs, fr)

    with_identity(work, out2[...])
    chol_inv(work, rows, {1: spread})
    l2, l2i = factors(rows)
    all_in(rest(slice(n, 2 * n)), vr_sem, gc[1])
    all_in(rest(slice(0, n)), fr, gc[1])

    avr[...] = mm(yw[:, 0:n], l2i, NT) + yw[:, n:]
    late.start_one()
    vr = mm(lead_ref[:, 0:n], l2i, NT) + jnp.where(eyes((height, n), row * height), 1.0, 0.0)
    src3[...] = mm(vr, avr[...], TN)
    red = Reduce(out3, red3[0], red3[1], red3[2:], ncol)
    red.start_first(src3)
    with_identity(work, mm(xt, l2i, NT).T + jnp.where(eyes((n, n)), 1.0, 0.0))
    near = (1, 3)
    gj_inverse(work, {4: red.start_second, 6: lambda: late.forward(0, near)})
    k = work[:, n:]

    def vectors(j):
        shift = (c * 4 + j) * height
        vc_ref[j] = mm(vc_ref[j], l2i, NT) + jnp.where(eyes((height, n), shift), 1.0, 0.0)
        put(vc_ref.at[j], vc_out.at[j])

    late.forward(1, near)
    red.start_c()
    late.forward(2, near)
    late.forward(3, near)
    vectors(0)
    late.relay(0)
    vectors(1)
    late.relay(1)
    vectors(2)
    late.relay(2)
    vectors(3)
    band_ref[...] = -mm(l2, l1_ref[...], (((0,), (1,)), ((), ())))
    put(band_ref, band_out)
    late.relay(3)
    red.finish()
    inner = mm(k, mm(out3[...], k), TN)
    right = jnp.concatenate([
        jnp.concatenate([jnp.zeros((n, n), F32), k], axis=1),
        jnp.concatenate([k.T, -0.5 * (inner + inner.T)], axis=1)], axis=0)
    lead_ref[...] = mm(jnp.concatenate([avr[...], vr], axis=1), right)
    put(lead_ref, lead_out)
    for j in range(4):
        at = late.nearest(j)
        late.relayed(at)
        put(avc_ref.at[at], avc_out.at[at])
    late.finish(2)
    for copy in outs:
        copy.wait()
    all_out(ybuf.at[1:ncol], ys, gc[1])
    all_out(rest(slice(0, n)), fs, gc[1])
    all_out(rest(slice(n, 2 * n)), vs, gc[1])

    @pl.when(c == 0)
    def _():
        all_out(rest(slice(0, n)), ws, gc[1])


def last_kernel(l1_in, band_in, lead_ref, avc_ref, vc_ref, a_ref, out_ref, band_ref, l1_ref, abuf, obuf, insem, outsem):
    width = avc_ref.shape[1]
    loads = [pltpu.make_async_copy(a_ref.at[:, k * width:(k + 1) * width], abuf.at[k], insem.at[k]) for k in range(4)]
    for copy in loads:
        copy.start()
    band_ref[...] = band_in[...]
    l1_ref[...] = l1_in[...]
    lead = halves(lead_ref[...])
    stores = []
    for k in range(4):
        tail = halves(jnp.concatenate([avc_ref[k], vc_ref[k]], axis=1))
        prod = mm3(lead, tail, NT)
        loads[k].wait()
        obuf[k] = abuf[k] - prod
        copy = pltpu.make_async_copy(obuf.at[k], out_ref.at[:, k * width:(k + 1) * width], outsem.at[k])
        copy.start()
        stores.append(copy)
    for copy in stores:
        copy.wait()


def body(ncol, panel, trailing):
    n = panel.shape[1]
    height, width = trailing.shape
    sl = height // ncol
    dma = pltpu.SemaphoreType.DMA

    def vmem(*shape):
        return pltpu.VMEM(shape, F32)

    l1, band, lead, avc, vc = pl.pallas_call(
        functools.partial(main_kernel, ncol),
        out_shape=(struct(n, n), struct(n, n), struct(height, 2 * n), struct(4, height, n), struct(4, height, n)),
        in_specs=[ANY, ANY], out_specs=(ANY,) * 5,
        scratch_shapes=[vmem(2 * n, n), vmem(2 * n, n), vmem(n, n), vmem(n, n), vmem(n, n), vmem(n, n)]
        + reduce_scratch(2 * n, ncol) + reduce_scratch(n, ncol) + reduce_scratch(n, ncol)
        + gather_sems() + gather_sems()
        + [vmem(height, width), vmem(4, height, n), vmem(n, 2 * n), vmem(n, 2 * n), vmem(height, n),
           vmem(ncol, sl, n), vmem(sl, n), vmem(height, 2 * n), vmem(height, n),
           vmem(height, n), vmem(n, n), vmem(n, n), vmem(height, 2 * n), vmem(4, height, n), vmem(4, height, n)]
        + [dma, dma, dma((11,)), dma, dma, dma, dma, dma, dma, dma, dma],
        compiler_params=pltpu.CompilerParams(collective_id=0, has_side_effects=True, vmem_limit_bytes=60 << 20),
        name="main")(panel, trailing)
    reduced, band, l1 = pl.pallas_call(
        last_kernel, out_shape=(struct(height, width), struct(n, n), struct(n, n)),
        in_specs=[VM] * 5 + [ANY], out_specs=(ANY, VM, VM),
        scratch_shapes=[vmem(4, height, width // 4), vmem(4, height, width // 4), dma((4,)), dma((4,))],
        compiler_params=pltpu.CompilerParams(vmem_limit_bytes=60 << 20), name="last",
    )(l1, band, lead, avc, vc, trailing)
    return reduced, band, l1


def solution(mesh):
    return jax.shard_map(
        functools.partial(body, mesh.shape["col"]), mesh=mesh, in_specs=(P("row", None), P("row", "col")),
        out_specs=(P("row", "col"), P(), P()), check_vma=False)
```

```python
import functools

import jax
import jax.numpy as jnp
from jax import lax
from jax.experimental import pallas as pl
from jax.experimental.pallas import tpu as pltpu
from jax.sharding import PartitionSpec as P

HIGH = lax.Precision.HIGHEST
F32 = jnp.float32
BF16 = jnp.bfloat16
MESH = pl.DeviceIdType.MESH
NX, NZ = 4, 8
BS = 16
NN = (((1,), (0,)), ((), ()))
NT = (((1,), (1,)), ((), ()))
TN = (((0,), (0,)), ((), ()))


def mm(a, b, dims=NN):
    return lax.dot_general(a, b, dims, precision=HIGH, preferred_element_type=F32)


def halves(a):
    top = a.astype(BF16)
    return top, (a - top.astype(F32)).astype(BF16)


def mm3(a, b, dims=NN):
    def one(p, q):
        return lax.dot_general(p, q, dims, preferred_element_type=F32)
    return one(a[0], b[0]) + (one(a[0], b[1]) + one(a[1], b[0]))


def eyes(shape, shift=0):
    return (lax.broadcasted_iota(jnp.int32, shape, 0) + shift) == lax.broadcasted_iota(jnp.int32, shape, 1)


def over(row, count):
    return jnp.broadcast_to(row, (count, row.shape[1]))


def eliminate(work, lo, hot, jordan):
    n = work.shape[0]
    bs = len(hot)
    rows = work[lo:lo + bs, :]
    col = [jnp.broadcast_to(rows[:, lo + k:lo + k + 1], (bs, n)) for k in range(bs)]
    pivots = []
    left, right = rows[:, 0:n], rows[:, n:]
    for t in range(bs):
        pivot = over(col[t][t:t + 1, :], bs)
        pivots.append(pivot[0:1, :])
        inv = 1.0 / pivot
        f = col[t] - hot[t] if jordan else jnp.where(hot[t], col[t], 0.0)
        for k in range(t + 1, bs):
            col[k] = col[k] - (f * over(col[k][t:t + 1, :], bs)) * inv
        g = f * inv
        left = left - g * over(left[t:t + 1, :], bs)
        right = right - g * over(right[t:t + 1, :], bs)
    return left, right, pivots


def chol_inv(work, rows, hooks=()):
    n = work.shape[0]
    at = lax.broadcasted_iota(jnp.int32, (BS, n), 0)
    hot = [at > t for t in range(BS)]
    for b in range(n // BS):
        lo = b * BS
        left, right, pivots = eliminate(work, lo, hot, False)
        scale = lax.rsqrt(jnp.concatenate(pivots, axis=0))
        blk = jnp.concatenate([left * scale, right * scale], axis=1)
        rows[lo:lo + BS, :] = blk
        if lo + BS < n:
            work[lo + BS:, :] = work[lo + BS:, :] - mm(blk[:, lo + BS:n], blk, TN)
        if b in hooks:
            hooks[b]()


def gj_inverse(work, hooks=()):
    n = work.shape[0]
    at = lax.broadcasted_iota(jnp.int32, (BS, n), 0)
    hot = [jnp.where(at == t, 1.0, 0.0) for t in range(BS)]
    for b in range(n // BS):
        lo = b * BS
        left, right, _ = eliminate(work, lo, hot, True)
        both = jnp.concatenate([left, right], axis=1)
        cols = work[:, lo:lo + BS]
        rowi = lax.broadcasted_iota(jnp.int32, cols.shape, 0)
        cols = jnp.where((rowi >= lo) & (rowi < lo + BS), 0.0, cols)
        work[...] = work[...] - mm(cols, both)
        work[lo:lo + BS, :] = both
        if b in hooks:
            hooks[b]()


def with_identity(work, square):
    n = work.shape[0]
    work[:, 0:n] = square
    work[:, n:] = jnp.where(eyes((n, n)), 1.0, 0.0)


def factors(rows):
    n = rows.shape[0]
    low = lax.broadcasted_iota(jnp.int32, (n, n), 0) >= lax.broadcasted_iota(jnp.int32, (n, n), 1)
    return jnp.where(low, rows[:, 0:n].T, 0.0), jnp.where(low, rows[:, n:], 0.0)


def place():
    row = lax.axis_index("row")
    return row // NZ, row % NZ, lax.axis_index("col")


def groups(ncol):
    x, z, c = place()
    gx = [(((x + d) % NX) * NZ + z, c) for d in range(NX)]
    gz = [(x * NZ + (z + d) % NZ, c) for d in range(NZ)]
    gc = [(x * NZ + z, (c + d) % ncol) for d in range(ncol)]
    return gx, gz, gc


def greet(ncol):
    sem = pltpu.get_barrier_semaphore()
    gx, gz, gc = groups(ncol)
    peers = gx[1:] + gz[1:] + gc[1:]
    for peer in peers:
        pl.semaphore_signal(sem, inc=1, device_id=peer, device_id_type=MESH)
    return sem, len(peers)


def send(src, dst, ss, rs, peer):
    copy = pltpu.make_async_remote_copy(
        src_ref=src, dst_ref=dst, send_sem=ss, recv_sem=rs, device_id=peer, device_id_type=MESH)
    copy.start()
    return copy


def slot_sum(buf, me, count):
    total = buf[me]
    for a in range(1, count):
        total = total + buf[(me + count - a) % count]
    return total


def all_in(view, sem, peer):
    pltpu.make_async_remote_copy(
        src_ref=view, dst_ref=view, send_sem=sem, recv_sem=sem, device_id=peer, device_id_type=MESH).wait_recv()


def all_out(view, sem, peer):
    pltpu.make_async_remote_copy(
        src_ref=view, dst_ref=view, send_sem=sem, recv_sem=sem, device_id=peer, device_id_type=MESH).wait_send()


class Reduce:
    def __init__(self, out, first, second, sems, ncol, z_first=False):
        self.out, self.first, self.second, self.ncol = out, first, second, ncol
        self.s1, self.r1, self.s2, self.r2, self.cs, self.cr = sems
        gx, gz, self.gc = groups(ncol)
        x, z, self.c = place()
        self.g1, self.g2 = (gz, gx) if z_first else (gx, gz)
        self.i1, self.i2 = (z, x) if z_first else (x, z)
        self.sl = out.shape[0] // ncol

    def part(self):
        return pl.ds(pl.multiple_of(self.c * self.sl, 8), self.sl)

    def start_first(self, src):
        self.first[0] = src[self.part(), :]
        for d in range(1, len(self.g1)):
            send(self.first.at[0], self.first.at[d], self.s1, self.r1, self.g1[d])

    def start_second(self):
        count = len(self.g1)
        all_in(self.first.at[1:count], self.r1, self.g1[1])
        self.second[0] = slot_sum(self.first, self.i1, count)
        for d in range(1, len(self.g2)):
            send(self.second.at[0], self.second.at[d], self.s2, self.r2, self.g2[d])

    def start_c(self):
        count = len(self.g2)
        all_in(self.second.at[1:count], self.r2, self.g2[1])
        self.out[self.part(), :] = slot_sum(self.second, self.i2, count)
        mine = self.out.at[self.part(), :]
        for d in range(1, self.ncol):
            send(mine, mine, self.cs, self.cr, self.gc[d])

    def finish(self):
        rest = self.out.at[0:(self.ncol - 1) * self.sl, :]
        all_in(rest, self.cr, self.gc[1])
        all_out(self.first.at[1:len(self.g1)], self.s1, self.g1[1])
        all_out(self.second.at[1:len(self.g2)], self.s2, self.g2[1])
        all_out(rest, self.cs, self.gc[1])


def reduce_scratch(height, ncol):
    sl = height // ncol
    dma = pltpu.SemaphoreType.DMA
    return [pltpu.VMEM((NX, sl, 128), F32), pltpu.VMEM((NZ, sl, 128), F32),
            dma, dma, dma, dma, dma, dma]


VM = pl.BlockSpec(memory_space=pltpu.VMEM)
ANY = pl.BlockSpec(memory_space=pl.ANY)


def comm_params(cid):
    return pltpu.CompilerParams(collective_id=cid, has_side_effects=True, vmem_limit_bytes=32 << 20)


def turn(y):
    return (y + 2) % 3 + y // 3


def unturn(t):
    return (t + 1) % 3 * (1 - t // 3) + 3 * (t // 3)


class Gather:
    def __init__(self, src, out, sems, ncol):
        self.src, self.out = src, out
        self.s1, self.r1, self.s2, self.r2, self.s3, self.r3 = sems
        self.x, self.z, self.c = place()
        y, core = self.c // 2, self.c % 2
        self.quarter = src.shape[0] // NX
        xd = (turn(y) + NX - self.x) % NX
        self.xd = xd
        self.to = [((xd * NZ) + 2 * j + core, self.x * 2 + self.z // 4) for j in range(4)]
        ys = unturn((self.x + y) % NX)
        self.frm = [(y * NZ + 4 * core + k, ys * 2 + self.z % 2) for k in range(4)]
        self.gx = groups(ncol)[0]

    def rows(self, x):
        return pl.ds(pl.multiple_of(x * self.quarter, 128), self.quarter)

    def start_one(self):
        k = self.z % 4
        for j in range(4):
            send(self.src.at[self.rows(self.xd), :], self.out.at[k, self.rows(self.xd), :],
                 self.s1, self.r1.at[k], self.to[j])

    def nearest(self, j):
        return (self.z + j) % 4

    def forward(self, j, steps=(1, 2, 3)):
        k = self.nearest(j)
        part = self.out.at[k, self.rows(self.x), :]
        all_in(part, self.r1.at[k], self.frm[0])
        for d in steps:
            send(part, part, self.s2, self.r2.at[k], self.gx[d])

    def relay(self, j):
        k = self.nearest(j)
        half = self.quarter // 2
        all_in(self.out.at[k, 0:2 * self.quarter, :], self.r2.at[k], self.gx[1])
        for i, d in enumerate((1, 3)):
            x = (self.x + NX - d) % NX
            part = self.out.at[k, pl.ds(pl.multiple_of(x * self.quarter + i * half, 8), half), :]
            send(part, part, self.s3, self.r3.at[k], self.gx[d])

    def block(self, k):
        all_in(self.out.at[k, 0:3 * self.quarter, :], self.r2.at[k], self.gx[1])

    def relayed(self, k):
        all_in(self.out.at[k, 0:self.quarter, :], self.r3.at[k], self.gx[1])

    def finish(self, near):
        all_out(self.out.at[:, 0:self.quarter, :], self.s1, self.to[0])
        all_out(self.out.at[:, 0:near * self.quarter, :], self.s2, self.gx[1])
        if near == 2:
            all_out(self.out.at[:, 0:self.quarter, :], self.s3, self.gx[1])


def gather_sems():
    dma = pltpu.SemaphoreType.DMA
    return [dma, dma((4,)), dma, dma((4,)), dma, dma((4,))]


VM = pl.BlockSpec(memory_space=pltpu.VMEM)
ANY = pl.BlockSpec(memory_space=pl.ANY)


def struct(*shape):
    return jax.ShapeDtypeStruct(shape, F32)


def main_kernel(ncol, p_hbm, a_ref, l1_ref, band_ref, lead_ref, avc_ref, vc_ref, av, *scratch):
    scratch = list(scratch)

    def take(count):
        head = scratch[:count]
        del scratch[:count]
        return head

    src1, out1, src2, out2, src3, out3 = take(6)
    red1, red2, red3 = take(8), take(8), take(8)
    gs1, gs2 = take(6), take(6)
    pc, work, rows, yp, ybuf, wbuf, yw, avr = take(8)
    p_ref, = take(1)
    asem, psem, ys, yr, ws, wr, vs, vr_sem, fs, fr = take(10)
    n = p_ref.shape[1]
    height = p_ref.shape[0]
    sl = height // ncol
    row, c = lax.axis_index("row"), lax.axis_index("col")

    sem, count = greet(ncol)
    early = Gather(p_ref, pc, gs1, ncol)
    late = Gather(avr, avc_ref, gs2, ncol)
    for peer in early.to + early.frm:
        pl.semaphore_signal(sem, inc=1, device_id=peer, device_id_type=MESH)
    count += len(early.to) + len(early.frm)
    fetch = pltpu.make_async_copy(p_hbm, p_ref, psem)
    fetch.start()
    load = pltpu.make_async_copy(a_ref, av, asem)
    load.start()
    fetch.wait()
    p = p_ref[...]
    src1[0:n, :] = mm(p, p, TN)
    src1[n:, :] = p[0:n, :] * jnp.where(row == 0, 1.0, 0.0)
    pl.semaphore_wait(sem, count)

    red = Reduce(out1, red1[0], red1[1], red1[2:], ncol)
    gc = red.gc
    red.start_first(src1)
    red.start_second()
    early.start_one()
    red.start_c()
    for j in range(4):
        early.forward(j)
    red.finish()

    def part(d):
        return pl.ds(pl.multiple_of(((c + d) % ncol) * sl, 8), sl)

    def wsend(d):
        return pltpu.make_async_remote_copy(
            src_ref=av.at[d * sl:(d + 1) * sl, 0:n], dst_ref=wbuf, send_sem=ws, recv_sem=wr,
            device_id=gc[d], device_id_type=MESH)

    def share(lanes, ssem, rsem):
        own = yw.at[part(0), lanes]
        for d in range(1, ncol):
            send(own, own, ssem, rsem, gc[d])

    def rest(lanes):
        return yw.at[0:(ncol - 1) * sl, lanes]

    load.wait()

    @pl.when(c == 0)
    def _():
        for d in range(1, ncol):
            wsend(d).start()
        wbuf[...] = av[0:sl, 0:n]

    with_identity(work, out1[0:n, :])
    chol_inv(work, rows)
    l1, l1i = factors(rows)

    xr = mm(p_ref[...], l1i, NT)
    src2[...] = mm(xr, xr, TN)
    red = Reduce(out2, red2[1], red2[0], red2[2:], ncol, z_first=True)
    red.start_first(src2)
    l1_ref[...] = l1
    lead_ref[:, 0:n] = xr
    xt = mm(out1[n:, :], l1i, NT)

    @pl.when(c != 0)
    def _():
        wsend(1).wait_recv()

    yw[part(0), n:] = wbuf[...]
    share(slice(n, 2 * n), vs, vr_sem)
    red.start_second()

    def block(k):
        early.block(k)
        xk = mm(pc[k], l1i, NT)
        vc_ref[k] = xk
        return mm3(halves(av[:, k * height:(k + 1) * height]), halves(xk))

    acc = block(0)
    acc = acc + block(1)
    acc = acc + block(2)
    red.start_c()
    acc = acc + block(3)
    yp[...] = acc
    early.finish(3)
    ybuf[0] = yp[part(0), :]
    for d in range(1, ncol):
        send(yp.at[part(d), :], ybuf.at[d], ys, yr, gc[d])
    red.finish()

    def spread():
        all_in(ybuf.at[1:ncol], yr, gc[1])
        yw[part(0), 0:n] = slot_sum(ybuf, c, ncol)
        share(slice(0, n), fs, fr)

    with_identity(work, out2[...])
    chol_inv(work, rows, {1: spread})
    l2, l2i = factors(rows)
    all_in(rest(slice(n, 2 * n)), vr_sem, gc[1])
    all_in(rest(slice(0, n)), fr, gc[1])

    avr[...] = mm(yw[:, 0:n], l2i, NT) + yw[:, n:]
    late.start_one()
    vr = mm(lead_ref[:, 0:n], l2i, NT) + jnp.where(eyes((height, n), row * height), 1.0, 0.0)
    src3[...] = mm(vr, avr[...], TN)
    red = Reduce(out3, red3[0], red3[1], red3[2:], ncol)
    red.start_first(src3)
    with_identity(work, mm(xt, l2i, NT).T + jnp.where(eyes((n, n)), 1.0, 0.0))
    near = (1, 3)
    gj_inverse(work, {4: red.start_second, 6: lambda: late.forward(0, near)})
    k = work[:, n:]

    def vectors(j):
        shift = (c * 4 + j) * height
        vc_ref[j] = mm(vc_ref[j], l2i, NT) + jnp.where(eyes((height, n), shift), 1.0, 0.0)

    late.forward(1, near)
    red.start_c()
    late.forward(2, near)
    late.forward(3, near)
    vectors(0)
    late.relay(0)
    vectors(1)
    late.relay(1)
    vectors(2)
    late.relay(2)
    vectors(3)
    band_ref[...] = -mm(l2, l1_ref[...], (((0,), (1,)), ((), ())))
    late.relay(3)
    red.finish()
    inner = mm(k, mm(out3[...], k), TN)
    right = jnp.concatenate([
        jnp.concatenate([jnp.zeros((n, n), F32), k], axis=1),
        jnp.concatenate([k.T, -0.5 * (inner + inner.T)], axis=1)], axis=0)
    lead_ref[...] = mm(jnp.concatenate([avr[...], vr], axis=1), right)
    for j in range(4):
        late.relayed(late.nearest(j))
    late.finish(2)
    all_out(ybuf.at[1:ncol], ys, gc[1])
    all_out(rest(slice(0, n)), fs, gc[1])
    all_out(rest(slice(n, 2 * n)), vs, gc[1])

    @pl.when(c == 0)
    def _():
        all_out(rest(slice(0, n)), ws, gc[1])


def last_kernel(l1_in, band_in, lead_ref, avc_ref, vc_ref, a_ref, out_ref, band_ref, l1_ref, obuf, outsem):
    width = avc_ref.shape[1]
    lead = halves(lead_ref[...])
    stores = []
    for k in range(4):
        cols = slice(k * width, (k + 1) * width)
        tail = halves(jnp.concatenate([avc_ref[k], vc_ref[k]], axis=1))
        obuf[k] = a_ref[:, cols] - mm3(lead, tail, NT)
        copy = pltpu.make_async_copy(obuf.at[k], out_ref.at[:, cols], outsem.at[k])
        copy.start()
        stores.append(copy)
    band_ref[...] = band_in[...]
    l1_ref[...] = l1_in[...]
    for copy in stores:
        copy.wait()


def body(ncol, panel, trailing):
    n = panel.shape[1]
    height, width = trailing.shape
    sl = height // ncol
    dma = pltpu.SemaphoreType.DMA

    def vmem(*shape):
        return pltpu.VMEM(shape, F32)

    l1, band, lead, avc, vc, kept = pl.pallas_call(
        functools.partial(main_kernel, ncol),
        out_shape=(vmem(n, n), vmem(n, n), vmem(height, 2 * n), vmem(4, height, n), vmem(4, height, n), vmem(height, width)),
        in_specs=[ANY, ANY], out_specs=(VM,) * 6,
        scratch_shapes=[vmem(2 * n, n), vmem(2 * n, n), vmem(n, n), vmem(n, n), vmem(n, n), vmem(n, n)]
        + reduce_scratch(2 * n, ncol) + reduce_scratch(n, ncol) + reduce_scratch(n, ncol)
        + gather_sems() + gather_sems()
        + [vmem(4, height, n), vmem(n, 2 * n), vmem(n, 2 * n), vmem(height, n),
           vmem(ncol, sl, n), vmem(sl, n), vmem(height, 2 * n), vmem(height, n),
           vmem(height, n)]
        + [dma, dma, dma, dma, dma, dma, dma, dma, dma, dma],
        compiler_params=pltpu.CompilerParams(collective_id=0, has_side_effects=True, vmem_limit_bytes=56 << 20),
        name="main")(panel, trailing)
    reduced, band, l1 = pl.pallas_call(
        last_kernel, out_shape=(struct(height, width), struct(n, n), struct(n, n)),
        in_specs=[VM] * 6, out_specs=(ANY, VM, VM),
        scratch_shapes=[vmem(4, height, width // 4), dma((4,))],
        compiler_params=pltpu.CompilerParams(vmem_limit_bytes=32 << 20), name="last",
    )(l1, band, lead, avc, vc, kept)
    return reduced, band, l1


def solution(mesh):
    return jax.shard_map(
        functools.partial(body, mesh.shape["col"]), mesh=mesh, in_specs=(P("row", None), P("row", "col")),
        out_specs=(P("row", "col"), P(), P()), check_vma=False)
```

```python
import functools

import jax
import jax.numpy as jnp
from jax import lax
from jax.experimental import pallas as pl
from jax.experimental.pallas import tpu as pltpu
from jax.sharding import PartitionSpec as P

HIGH = lax.Precision.HIGHEST
F32 = jnp.float32
BF16 = jnp.bfloat16
MESH = pl.DeviceIdType.MESH
NX, NZ = 4, 8
BS = 16
NN = (((1,), (0,)), ((), ()))
NT = (((1,), (1,)), ((), ()))
TN = (((0,), (0,)), ((), ()))


def mm(a, b, dims=NN):
    return lax.dot_general(a, b, dims, precision=HIGH, preferred_element_type=F32)


def halves(a):
    top = a.astype(BF16)
    return top, (a - top.astype(F32)).astype(BF16)


def mm3(a, b, dims=NN):
    def one(p, q):
        return lax.dot_general(p, q, dims, preferred_element_type=F32)
    return one(a[0], b[0]) + (one(a[0], b[1]) + one(a[1], b[0]))


def eyes(shape, shift=0):
    return (lax.broadcasted_iota(jnp.int32, shape, 0) + shift) == lax.broadcasted_iota(jnp.int32, shape, 1)


def over(row, count):
    return jnp.broadcast_to(row, (count, row.shape[1]))


def eliminate(work, lo, hot, jordan):
    n = work.shape[0]
    bs = len(hot)
    rows = work[lo:lo + bs, :]
    col = [jnp.broadcast_to(rows[:, lo + k:lo + k + 1], (bs, n)) for k in range(bs)]
    pivots = []
    left, right = rows[:, 0:n], rows[:, n:]
    for t in range(bs):
        pivot = over(col[t][t:t + 1, :], bs)
        pivots.append(pivot[0:1, :])
        inv = 1.0 / pivot
        f = col[t] - hot[t] if jordan else jnp.where(hot[t], col[t], 0.0)
        for k in range(t + 1, bs):
            col[k] = col[k] - (f * over(col[k][t:t + 1, :], bs)) * inv
        g = f * inv
        left = left - g * over(left[t:t + 1, :], bs)
        right = right - g * over(right[t:t + 1, :], bs)
    return left, right, pivots


def chol_inv(work, rows, hooks=()):
    n = work.shape[0]
    at = lax.broadcasted_iota(jnp.int32, (BS, n), 0)
    hot = [at > t for t in range(BS)]
    for b in range(n // BS):
        lo = b * BS
        left, right, pivots = eliminate(work, lo, hot, False)
        scale = lax.rsqrt(jnp.concatenate(pivots, axis=0))
        blk = jnp.concatenate([left * scale, right * scale], axis=1)
        rows[lo:lo + BS, :] = blk
        if lo + BS < n:
            work[lo + BS:, :] = work[lo + BS:, :] - mm(blk[:, lo + BS:n], blk, TN)
        if b in hooks:
            hooks[b]()


def gj_inverse(work, hooks=()):
    n = work.shape[0]
    at = lax.broadcasted_iota(jnp.int32, (BS, n), 0)
    hot = [jnp.where(at == t, 1.0, 0.0) for t in range(BS)]
    for b in range(n // BS):
        lo = b * BS
        left, right, _ = eliminate(work, lo, hot, True)
        both = jnp.concatenate([left, right], axis=1)
        cols = work[:, lo:lo + BS]
        rowi = lax.broadcasted_iota(jnp.int32, cols.shape, 0)
        cols = jnp.where((rowi >= lo) & (rowi < lo + BS), 0.0, cols)
        work[...] = work[...] - mm(cols, both)
        work[lo:lo + BS, :] = both
        if b in hooks:
            hooks[b]()


def with_identity(work, square):
    n = work.shape[0]
    work[:, 0:n] = square
    work[:, n:] = jnp.where(eyes((n, n)), 1.0, 0.0)


def factors(rows):
    n = rows.shape[0]
    low = lax.broadcasted_iota(jnp.int32, (n, n), 0) >= lax.broadcasted_iota(jnp.int32, (n, n), 1)
    return jnp.where(low, rows[:, 0:n].T, 0.0), jnp.where(low, rows[:, n:], 0.0)


def place():
    row = lax.axis_index("row")
    return row // NZ, row % NZ, lax.axis_index("col")


def groups(ncol):
    x, z, c = place()
    gx = [(((x + d) % NX) * NZ + z, c) for d in range(NX)]
    gz = [(x * NZ + (z + d) % NZ, c) for d in range(NZ)]
    gc = [(x * NZ + z, (c + d) % ncol) for d in range(ncol)]
    return gx, gz, gc


def greet(ncol):
    sem = pltpu.get_barrier_semaphore()
    gx, gz, gc = groups(ncol)
    peers = gx[1:] + gz[1:] + gc[1:]
    for peer in peers:
        pl.semaphore_signal(sem, inc=1, device_id=peer, device_id_type=MESH)
    return sem, len(peers)


def send(src, dst, ss, rs, peer):
    copy = pltpu.make_async_remote_copy(
        src_ref=src, dst_ref=dst, send_sem=ss, recv_sem=rs, device_id=peer, device_id_type=MESH)
    copy.start()
    return copy


def slot_sum(buf, me, count):
    total = buf[me]
    for a in range(1, count):
        total = total + buf[(me + count - a) % count]
    return total


def all_in(view, sem, peer):
    pltpu.make_async_remote_copy(
        src_ref=view, dst_ref=view, send_sem=sem, recv_sem=sem, device_id=peer, device_id_type=MESH).wait_recv()


def all_out(view, sem, peer):
    pltpu.make_async_remote_copy(
        src_ref=view, dst_ref=view, send_sem=sem, recv_sem=sem, device_id=peer, device_id_type=MESH).wait_send()


class Reduce:
    def __init__(self, out, first, second, sems, ncol, z_first=False):
        self.out, self.first, self.second, self.ncol = out, first, second, ncol
        self.s1, self.r1, self.s2, self.r2, self.cs, self.cr = sems
        gx, gz, self.gc = groups(ncol)
        x, z, self.c = place()
        self.g1, self.g2 = (gz, gx) if z_first else (gx, gz)
        self.i1, self.i2 = (z, x) if z_first else (x, z)
        self.sl = out.shape[0] // ncol

    def part(self):
        return pl.ds(pl.multiple_of(self.c * self.sl, 8), self.sl)

    def start_first(self, src):
        self.first[0] = src[self.part(), :]
        for d in range(1, len(self.g1)):
            send(self.first.at[0], self.first.at[d], self.s1, self.r1, self.g1[d])

    def start_second(self):
        count = len(self.g1)
        all_in(self.first.at[1:count], self.r1, self.g1[1])
        self.second[0] = slot_sum(self.first, self.i1, count)
        for d in range(1, len(self.g2)):
            send(self.second.at[0], self.second.at[d], self.s2, self.r2, self.g2[d])

    def start_c(self):
        count = len(self.g2)
        all_in(self.second.at[1:count], self.r2, self.g2[1])
        self.out[self.part(), :] = slot_sum(self.second, self.i2, count)
        mine = self.out.at[self.part(), :]
        for d in range(1, self.ncol):
            send(mine, mine, self.cs, self.cr, self.gc[d])

    def finish(self):
        rest = self.out.at[0:(self.ncol - 1) * self.sl, :]
        all_in(rest, self.cr, self.gc[1])
        all_out(self.first.at[1:len(self.g1)], self.s1, self.g1[1])
        all_out(self.second.at[1:len(self.g2)], self.s2, self.g2[1])
        all_out(rest, self.cs, self.gc[1])


def reduce_scratch(height, ncol):
    sl = height // ncol
    dma = pltpu.SemaphoreType.DMA
    return [pltpu.VMEM((NX, sl, 128), F32), pltpu.VMEM((NZ, sl, 128), F32),
            dma, dma, dma, dma, dma, dma]


VM = pl.BlockSpec(memory_space=pltpu.VMEM)
ANY = pl.BlockSpec(memory_space=pl.ANY)


def comm_params(cid):
    return pltpu.CompilerParams(collective_id=cid, has_side_effects=True, vmem_limit_bytes=32 << 20)


def turn(y):
    return (y + 2) % 3 + y // 3


def unturn(t):
    return (t + 1) % 3 * (1 - t // 3) + 3 * (t // 3)


class Gather:
    def __init__(self, src, out, sems, ncol):
        self.src, self.out = src, out
        self.s1, self.r1, self.s2, self.r2, self.s3, self.r3 = sems
        self.x, self.z, self.c = place()
        y, core = self.c // 2, self.c % 2
        self.quarter = src.shape[0] // NX
        xd = (turn(y) + NX - self.x) % NX
        self.xd = xd
        self.to = [((xd * NZ) + 2 * j + core, self.x * 2 + self.z // 4) for j in range(4)]
        ys = unturn((self.x + y) % NX)
        self.frm = [(y * NZ + 4 * core + k, ys * 2 + self.z % 2) for k in range(4)]
        self.gx = groups(ncol)[0]

    def rows(self, x):
        return pl.ds(pl.multiple_of(x * self.quarter, 128), self.quarter)

    def start_one(self):
        k = self.z % 4
        for j in range(4):
            send(self.src.at[self.rows(self.xd), :], self.out.at[k, self.rows(self.xd), :],
                 self.s1, self.r1.at[k], self.to[j])

    def nearest(self, j):
        return (self.z + j) % 4

    def forward(self, j, steps=(1, 2, 3)):
        k = self.nearest(j)
        part = self.out.at[k, self.rows(self.x), :]
        all_in(part, self.r1.at[k], self.frm[0])
        for d in steps:
            send(part, part, self.s2, self.r2.at[k], self.gx[d])

    def relay(self, j):
        k = self.nearest(j)
        half = self.quarter // 2
        all_in(self.out.at[k, 0:2 * self.quarter, :], self.r2.at[k], self.gx[1])
        for i, d in enumerate((1, 3)):
            x = (self.x + NX - d) % NX
            part = self.out.at[k, pl.ds(pl.multiple_of(x * self.quarter + i * half, 8), half), :]
            send(part, part, self.s3, self.r3.at[k], self.gx[d])

    def block(self, k):
        all_in(self.out.at[k, 0:3 * self.quarter, :], self.r2.at[k], self.gx[1])

    def relayed(self, k):
        all_in(self.out.at[k, 0:self.quarter, :], self.r3.at[k], self.gx[1])

    def finish(self, near):
        all_out(self.out.at[:, 0:self.quarter, :], self.s1, self.to[0])
        all_out(self.out.at[:, 0:near * self.quarter, :], self.s2, self.gx[1])
        if near == 2:
            all_out(self.out.at[:, 0:self.quarter, :], self.s3, self.gx[1])


def gather_sems():
    dma = pltpu.SemaphoreType.DMA
    return [dma, dma((4,)), dma, dma((4,)), dma, dma((4,))]


VM = pl.BlockSpec(memory_space=pltpu.VMEM)
ANY = pl.BlockSpec(memory_space=pl.ANY)


def struct(*shape):
    return jax.ShapeDtypeStruct(shape, F32)


def main_kernel(ncol, p_hbm, a_ref, l1_ref, band_ref, lead_ref, avc_ref, vc_ref, av, *scratch):
    scratch = list(scratch)

    def take(count):
        head = scratch[:count]
        del scratch[:count]
        return head

    src1, out1, src2, out2, src3, out3 = take(6)
    red1, red2, red3 = take(8), take(8), take(8)
    gs1, gs2 = take(6), take(6)
    pc, work, rows, yp, ybuf, wbuf, yw, avr = take(8)
    p_ref, = take(1)
    asem, psem, ys, yr, ws, wr, vs, vr_sem, fs, fr = take(10)
    n = p_ref.shape[1]
    height = p_ref.shape[0]
    sl = height // ncol
    row, c = lax.axis_index("row"), lax.axis_index("col")

    sem, count = greet(ncol)
    early = Gather(p_ref, pc, gs1, ncol)
    late = Gather(avr, avc_ref, gs2, ncol)
    for peer in early.to + early.frm:
        pl.semaphore_signal(sem, inc=1, device_id=peer, device_id_type=MESH)
    count += len(early.to) + len(early.frm)
    fetch = pltpu.make_async_copy(p_hbm, p_ref, psem)
    fetch.start()
    load = pltpu.make_async_copy(a_ref, av, asem)
    load.start()
    fetch.wait()
    p = p_ref[...]
    src1[0:n, :] = mm(p, p, TN)
    src1[n:, :] = p[0:n, :] * jnp.where(row == 0, 1.0, 0.0)
    pl.semaphore_wait(sem, count)

    red = Reduce(out1, red1[0], red1[1], red1[2:], ncol)
    gc = red.gc
    red.start_first(src1)
    red.start_second()
    early.start_one()
    red.start_c()
    red.finish()

    def part(d):
        return pl.ds(pl.multiple_of(((c + d) % ncol) * sl, 8), sl)

    def wsend(d):
        return pltpu.make_async_remote_copy(
            src_ref=av.at[d * sl:(d + 1) * sl, 0:n], dst_ref=wbuf, send_sem=ws, recv_sem=wr,
            device_id=gc[d], device_id_type=MESH)

    def share(lanes, ssem, rsem):
        own = yw.at[part(0), lanes]
        for d in range(1, ncol):
            send(own, own, ssem, rsem, gc[d])

    def rest(lanes):
        return yw.at[0:(ncol - 1) * sl, lanes]

    load.wait()

    @pl.when(c == 0)
    def _():
        for d in range(1, ncol):
            wsend(d).start()
        wbuf[...] = av[0:sl, 0:n]

    with_identity(work, out1[0:n, :])
    chol_inv(work, rows, {j: functools.partial(early.forward, j) for j in range(4)})
    l1, l1i = factors(rows)

    xr = mm(p_ref[...], l1i, NT)
    src2[...] = mm(xr, xr, TN)
    red = Reduce(out2, red2[1], red2[0], red2[2:], ncol, z_first=True)
    red.start_first(src2)
    l1_ref[...] = l1
    lead_ref[:, 0:n] = xr
    xt = mm(out1[n:, :], l1i, NT)

    @pl.when(c != 0)
    def _():
        wsend(1).wait_recv()

    yw[part(0), n:] = wbuf[...]
    share(slice(n, 2 * n), vs, vr_sem)

    def block(j):
        k = early.nearest(j)
        early.block(k)
        xk = mm(pc[k], l1i, NT)
        vc_ref[k] = xk
        return mm3(halves(av[:, pl.ds(pl.multiple_of(k * height, 128), height)]), halves(xk))

    acc = block(0)
    acc = acc + block(1)
    red.start_second()
    acc = acc + block(2)
    acc = acc + block(3)
    yp[...] = acc
    red.start_c()
    ybuf[0] = yp[part(0), :]
    for d in range(1, ncol):
        send(yp.at[part(d), :], ybuf.at[d], ys, yr, gc[d])
    early.finish(3)
    red.finish()

    def spread():
        all_in(ybuf.at[1:ncol], yr, gc[1])
        yw[part(0), 0:n] = slot_sum(ybuf, c, ncol)
        share(slice(0, n), fs, fr)

    with_identity(work, out2[...])
    chol_inv(work, rows, {1: spread})
    l2, l2i = factors(rows)
    all_in(rest(slice(n, 2 * n)), vr_sem, gc[1])
    all_in(rest(slice(0, n)), fr, gc[1])

    avr[...] = mm(yw[:, 0:n], l2i, NT) + yw[:, n:]
    late.start_one()
    vr = mm(lead_ref[:, 0:n], l2i, NT) + jnp.where(eyes((height, n), row * height), 1.0, 0.0)
    src3[...] = mm(vr, avr[...], TN)
    red = Reduce(out3, red3[0], red3[1], red3[2:], ncol)
    red.start_first(src3)
    with_identity(work, mm(xt, l2i, NT).T + jnp.where(eyes((n, n)), 1.0, 0.0))
    near = (1, 3)
    gj_inverse(work, {4: red.start_second, 6: lambda: late.forward(0, near)})
    k = work[:, n:]

    def vectors(j):
        shift = (c * 4 + j) * height
        vc_ref[j] = mm(vc_ref[j], l2i, NT) + jnp.where(eyes((height, n), shift), 1.0, 0.0)

    late.forward(1, near)
    red.start_c()
    late.forward(2, near)
    late.forward(3, near)
    vectors(0)
    late.relay(0)
    vectors(1)
    late.relay(1)
    vectors(2)
    late.relay(2)
    vectors(3)
    band_ref[...] = -mm(l2, l1_ref[...], (((0,), (1,)), ((), ())))
    late.relay(3)
    red.finish()
    inner = mm(k, mm(out3[...], k), TN)
    right = jnp.concatenate([
        jnp.concatenate([jnp.zeros((n, n), F32), k], axis=1),
        jnp.concatenate([k.T, -0.5 * (inner + inner.T)], axis=1)], axis=0)
    lead_ref[...] = mm(jnp.concatenate([avr[...], vr], axis=1), right)
    for j in range(4):
        late.relayed(late.nearest(j))
    late.finish(2)
    all_out(ybuf.at[1:ncol], ys, gc[1])
    all_out(rest(slice(0, n)), fs, gc[1])
    all_out(rest(slice(n, 2 * n)), vs, gc[1])

    @pl.when(c == 0)
    def _():
        all_out(rest(slice(0, n)), ws, gc[1])


def last_kernel(l1_in, band_in, lead_ref, avc_ref, vc_ref, a_ref, out_ref, band_ref, l1_ref, obuf, outsem):
    width = avc_ref.shape[1]
    lead = halves(lead_ref[...])
    stores = []
    for k in range(4):
        cols = slice(k * width, (k + 1) * width)
        tail = halves(jnp.concatenate([avc_ref[k], vc_ref[k]], axis=1))
        obuf[k] = a_ref[:, cols] - mm3(lead, tail, NT)
        copy = pltpu.make_async_copy(obuf.at[k], out_ref.at[:, cols], outsem.at[k])
        copy.start()
        stores.append(copy)
    band_ref[...] = band_in[...]
    l1_ref[...] = l1_in[...]
    for copy in stores:
        copy.wait()


def body(ncol, panel, trailing):
    n = panel.shape[1]
    height, width = trailing.shape
    sl = height // ncol
    dma = pltpu.SemaphoreType.DMA

    def vmem(*shape):
        return pltpu.VMEM(shape, F32)

    l1, band, lead, avc, vc, kept = pl.pallas_call(
        functools.partial(main_kernel, ncol),
        out_shape=(vmem(n, n), vmem(n, n), vmem(height, 2 * n), vmem(4, height, n), vmem(4, height, n), vmem(height, width)),
        in_specs=[ANY, ANY], out_specs=(VM,) * 6,
        scratch_shapes=[vmem(2 * n, n), vmem(2 * n, n), vmem(n, n), vmem(n, n), vmem(n, n), vmem(n, n)]
        + reduce_scratch(2 * n, ncol) + reduce_scratch(n, ncol) + reduce_scratch(n, ncol)
        + gather_sems() + gather_sems()
        + [vmem(4, height, n), vmem(n, 2 * n), vmem(n, 2 * n), vmem(height, n),
           vmem(ncol, sl, n), vmem(sl, n), vmem(height, 2 * n), vmem(height, n),
           vmem(height, n)]
        + [dma, dma, dma, dma, dma, dma, dma, dma, dma, dma],
        compiler_params=pltpu.CompilerParams(collective_id=0, has_side_effects=True, vmem_limit_bytes=56 << 20),
        name="main")(panel, trailing)
    reduced, band, l1 = pl.pallas_call(
        last_kernel, out_shape=(struct(height, width), struct(n, n), struct(n, n)),
        in_specs=[VM] * 6, out_specs=(ANY, VM, VM),
        scratch_shapes=[vmem(4, height, width // 4), dma((4,))],
        compiler_params=pltpu.CompilerParams(vmem_limit_bytes=32 << 20), name="last",
    )(l1, band, lead, avc, vc, kept)
    return reduced, band, l1


def solution(mesh):
    return jax.shard_map(
        functools.partial(body, mesh.shape["col"]), mesh=mesh, in_specs=(P("row", None), P("row", "col")),
        out_specs=(P("row", "col"), P(), P()), check_vma=False)
```

```python
import functools

import jax
import jax.numpy as jnp
from jax import lax
from jax.experimental import pallas as pl
from jax.experimental.pallas import tpu as pltpu
from jax.sharding import PartitionSpec as P

HIGH = lax.Precision.HIGHEST
F32 = jnp.float32
BF16 = jnp.bfloat16
MESH = pl.DeviceIdType.MESH
NX, NZ = 4, 8
BS = 16
NN = (((1,), (0,)), ((), ()))
NT = (((1,), (1,)), ((), ()))
TN = (((0,), (0,)), ((), ()))


def mm(a, b, dims=NN):
    return lax.dot_general(a, b, dims, precision=HIGH, preferred_element_type=F32)


def halves(a):
    top = a.astype(BF16)
    return top, (a - top.astype(F32)).astype(BF16)


def mm3(a, b, dims=NN):
    def one(p, q):
        return lax.dot_general(p, q, dims, preferred_element_type=F32)
    return one(a[0], b[0]) + (one(a[0], b[1]) + one(a[1], b[0]))


def eyes(shape, shift=0):
    return (lax.broadcasted_iota(jnp.int32, shape, 0) + shift) == lax.broadcasted_iota(jnp.int32, shape, 1)


def over(row, count):
    return jnp.broadcast_to(row, (count, row.shape[1]))


def eliminate(work, lo, hot, jordan):
    n = work.shape[0]
    bs = len(hot)
    rows = work[lo:lo + bs, :]
    col = [jnp.broadcast_to(rows[:, lo + k:lo + k + 1], (bs, n)) for k in range(bs)]
    pivots = []
    left, right = rows[:, 0:n], rows[:, n:]
    for t in range(bs):
        pivot = over(col[t][t:t + 1, :], bs)
        pivots.append(pivot[0:1, :])
        inv = 1.0 / pivot
        f = col[t] - hot[t] if jordan else jnp.where(hot[t], col[t], 0.0)
        for k in range(t + 1, bs):
            col[k] = col[k] - (f * over(col[k][t:t + 1, :], bs)) * inv
        g = f * inv
        left = left - g * over(left[t:t + 1, :], bs)
        right = right - g * over(right[t:t + 1, :], bs)
    return left, right, pivots


def chol_inv(work, rows, hooks=()):
    n = work.shape[0]
    at = lax.broadcasted_iota(jnp.int32, (BS, n), 0)
    hot = [at > t for t in range(BS)]
    for b in range(n // BS):
        lo = b * BS
        left, right, pivots = eliminate(work, lo, hot, False)
        scale = lax.rsqrt(jnp.concatenate(pivots, axis=0))
        blk = jnp.concatenate([left * scale, right * scale], axis=1)
        rows[lo:lo + BS, :] = blk
        if lo + BS < n:
            work[lo + BS:, :] = work[lo + BS:, :] - mm(blk[:, lo + BS:n], blk, TN)
        if b in hooks:
            hooks[b]()


def gj_inverse(work, hooks=()):
    n = work.shape[0]
    at = lax.broadcasted_iota(jnp.int32, (BS, n), 0)
    hot = [jnp.where(at == t, 1.0, 0.0) for t in range(BS)]
    for b in range(n // BS):
        lo = b * BS
        left, right, _ = eliminate(work, lo, hot, True)
        both = jnp.concatenate([left, right], axis=1)
        cols = work[:, lo:lo + BS]
        rowi = lax.broadcasted_iota(jnp.int32, cols.shape, 0)
        cols = jnp.where((rowi >= lo) & (rowi < lo + BS), 0.0, cols)
        work[...] = work[...] - mm(cols, both)
        work[lo:lo + BS, :] = both
        if b in hooks:
            hooks[b]()


def with_identity(work, square):
    n = work.shape[0]
    work[:, 0:n] = square
    work[:, n:] = jnp.where(eyes((n, n)), 1.0, 0.0)


def factors(rows):
    n = rows.shape[0]
    low = lax.broadcasted_iota(jnp.int32, (n, n), 0) >= lax.broadcasted_iota(jnp.int32, (n, n), 1)
    return jnp.where(low, rows[:, 0:n].T, 0.0), jnp.where(low, rows[:, n:], 0.0)


def place():
    row = lax.axis_index("row")
    return row // NZ, row % NZ, lax.axis_index("col")


def groups(ncol):
    x, z, c = place()
    gx = [(((x + d) % NX) * NZ + z, c) for d in range(NX)]
    gz = [(x * NZ + (z + d) % NZ, c) for d in range(NZ)]
    gc = [(x * NZ + z, (c + d) % ncol) for d in range(ncol)]
    return gx, gz, gc


def greet(ncol):
    sem = pltpu.get_barrier_semaphore()
    gx, gz, gc = groups(ncol)
    peers = gx[1:] + gz[1:] + gc[1:]
    for peer in peers:
        pl.semaphore_signal(sem, inc=1, device_id=peer, device_id_type=MESH)
    return sem, len(peers)


def send(src, dst, ss, rs, peer):
    copy = pltpu.make_async_remote_copy(
        src_ref=src, dst_ref=dst, send_sem=ss, recv_sem=rs, device_id=peer, device_id_type=MESH)
    copy.start()
    return copy


def slot_sum(buf, me, count):
    total = buf[me]
    for a in range(1, count):
        total = total + buf[(me + count - a) % count]
    return total


def all_in(view, sem, peer):
    pltpu.make_async_remote_copy(
        src_ref=view, dst_ref=view, send_sem=sem, recv_sem=sem, device_id=peer, device_id_type=MESH).wait_recv()


def all_out(view, sem, peer):
    pltpu.make_async_remote_copy(
        src_ref=view, dst_ref=view, send_sem=sem, recv_sem=sem, device_id=peer, device_id_type=MESH).wait_send()


class Reduce:
    def __init__(self, out, first, second, sems, ncol, z_first=False):
        self.out, self.first, self.second, self.ncol = out, first, second, ncol
        self.s1, self.r1, self.s2, self.r2, self.cs, self.cr = sems
        gx, gz, self.gc = groups(ncol)
        x, z, self.c = place()
        self.g1, self.g2 = (gz, gx) if z_first else (gx, gz)
        self.i1, self.i2 = (z, x) if z_first else (x, z)
        self.sl = out.shape[0] // ncol

    def part(self):
        return pl.ds(pl.multiple_of(self.c * self.sl, 8), self.sl)

    def start_first(self, src):
        self.first[0] = src[self.part(), :]
        for d in range(1, len(self.g1)):
            send(self.first.at[0], self.first.at[d], self.s1, self.r1, self.g1[d])

    def start_second(self):
        count = len(self.g1)
        all_in(self.first.at[1:count], self.r1, self.g1[1])
        self.second[0] = slot_sum(self.first, self.i1, count)
        for d in range(1, len(self.g2)):
            send(self.second.at[0], self.second.at[d], self.s2, self.r2, self.g2[d])

    def start_c(self):
        count = len(self.g2)
        all_in(self.second.at[1:count], self.r2, self.g2[1])
        self.out[self.part(), :] = slot_sum(self.second, self.i2, count)
        mine = self.out.at[self.part(), :]
        for d in range(1, self.ncol):
            send(mine, mine, self.cs, self.cr, self.gc[d])

    def finish(self):
        rest = self.out.at[0:(self.ncol - 1) * self.sl, :]
        all_in(rest, self.cr, self.gc[1])
        all_out(self.first.at[1:len(self.g1)], self.s1, self.g1[1])
        all_out(self.second.at[1:len(self.g2)], self.s2, self.g2[1])
        all_out(rest, self.cs, self.gc[1])


def reduce_scratch(height, ncol):
    sl = height // ncol
    dma = pltpu.SemaphoreType.DMA
    return [pltpu.VMEM((NX, sl, 128), F32), pltpu.VMEM((NZ, sl, 128), F32),
            dma, dma, dma, dma, dma, dma]


VM = pl.BlockSpec(memory_space=pltpu.VMEM)
ANY = pl.BlockSpec(memory_space=pl.ANY)


def comm_params(cid):
    return pltpu.CompilerParams(collective_id=cid, has_side_effects=True, vmem_limit_bytes=32 << 20)


def turn(y):
    return (y + 2) % 3 + y // 3


def unturn(t):
    return (t + 1) % 3 * (1 - t // 3) + 3 * (t // 3)


class Gather:
    def __init__(self, src, out, sems, ncol):
        self.src, self.out = src, out
        self.s1, self.r1, self.s2, self.r2, self.s3, self.r3 = sems
        self.x, self.z, self.c = place()
        y, core = self.c // 2, self.c % 2
        self.quarter = src.shape[0] // NX
        xd = (turn(y) + NX - self.x) % NX
        self.xd = xd
        self.to = [((xd * NZ) + 2 * j + core, self.x * 2 + self.z // 4) for j in range(4)]
        ys = unturn((self.x + y) % NX)
        self.frm = [(y * NZ + 4 * core + k, ys * 2 + self.z % 2) for k in range(4)]
        self.gx = groups(ncol)[0]

    def rows(self, x):
        return pl.ds(pl.multiple_of(x * self.quarter, 128), self.quarter)

    def start_one(self):
        k = self.z % 4
        for j in range(4):
            send(self.src.at[self.rows(self.xd), :], self.out.at[k, self.rows(self.xd), :],
                 self.s1, self.r1.at[k], self.to[j])

    def nearest(self, j):
        return (self.z + j) % 4

    def forward(self, j, steps=(1, 2, 3)):
        k = self.nearest(j)
        part = self.out.at[k, self.rows(self.x), :]
        all_in(part, self.r1.at[k], self.frm[0])
        for d in steps:
            send(part, part, self.s2, self.r2.at[k], self.gx[d])

    def relay(self, j):
        k = self.nearest(j)
        half = self.quarter // 2
        all_in(self.out.at[k, 0:2 * self.quarter, :], self.r2.at[k], self.gx[1])
        for i, d in enumerate((1, 3)):
            x = (self.x + NX - d) % NX
            part = self.out.at[k, pl.ds(pl.multiple_of(x * self.quarter + i * half, 8), half), :]
            send(part, part, self.s3, self.r3.at[k], self.gx[d])

    def block(self, k):
        all_in(self.out.at[k, 0:3 * self.quarter, :], self.r2.at[k], self.gx[1])

    def relayed(self, k):
        all_in(self.out.at[k, 0:self.quarter, :], self.r3.at[k], self.gx[1])

    def finish(self, near):
        all_out(self.out.at[:, 0:self.quarter, :], self.s1, self.to[0])
        all_out(self.out.at[:, 0:near * self.quarter, :], self.s2, self.gx[1])
        if near == 2:
            all_out(self.out.at[:, 0:self.quarter, :], self.s3, self.gx[1])


def gather_sems():
    dma = pltpu.SemaphoreType.DMA
    return [dma, dma((4,)), dma, dma((4,)), dma, dma((4,))]


VM = pl.BlockSpec(memory_space=pltpu.VMEM)
ANY = pl.BlockSpec(memory_space=pl.ANY)


def struct(*shape):
    return jax.ShapeDtypeStruct(shape, F32)


def main_kernel(ncol, p_hbm, a_ref, l1_ref, band_ref, lead_ref, avc_ref, vc_ref, av, *scratch):
    scratch = list(scratch)

    def take(count):
        head = scratch[:count]
        del scratch[:count]
        return head

    src1, out1, src2, out2, src3, out3 = take(6)
    red1, red2, red3 = take(8), take(8), take(8)
    gs1, gs2 = take(6), take(6)
    pc, work, rows, yp, ybuf, wbuf, yw, avr = take(8)
    p_ref, = take(1)
    asem, psem, ys, yr, ws, wr, vs, vr_sem, fs, fr = take(10)
    n = p_ref.shape[1]
    height = p_ref.shape[0]
    sl = height // ncol
    row, c = lax.axis_index("row"), lax.axis_index("col")

    sem, count = greet(ncol)
    early = Gather(p_ref, pc, gs1, ncol)
    late = Gather(avr, avc_ref, gs2, ncol)
    for peer in early.to + early.frm:
        pl.semaphore_signal(sem, inc=1, device_id=peer, device_id_type=MESH)
    count += len(early.to) + len(early.frm)
    fetch = pltpu.make_async_copy(p_hbm, p_ref, psem)
    fetch.start()
    load = pltpu.make_async_copy(a_ref, av, asem)
    load.start()
    fetch.wait()
    p = p_ref[...]
    src1[0:n, :] = mm(p, p, TN)
    src1[n:, :] = p[0:n, :] * jnp.where(row == 0, 1.0, 0.0)
    pl.semaphore_wait(sem, count)

    red = Reduce(out1, red1[0], red1[1], red1[2:], ncol)
    gc = red.gc
    red.start_first(src1)
    red.start_second()
    early.start_one()
    red.start_c()
    red.finish()

    def part(d):
        return pl.ds(pl.multiple_of(((c + d) % ncol) * sl, 8), sl)

    def wsend(d):
        return pltpu.make_async_remote_copy(
            src_ref=av.at[d * sl:(d + 1) * sl, 0:n], dst_ref=wbuf, send_sem=ws, recv_sem=wr,
            device_id=gc[d], device_id_type=MESH)

    def share(lanes, ssem, rsem):
        own = yw.at[part(0), lanes]
        for d in range(1, ncol):
            send(own, own, ssem, rsem, gc[d])

    def rest(lanes):
        return yw.at[0:(ncol - 1) * sl, lanes]

    load.wait()

    @pl.when(c == 0)
    def _():
        for d in range(1, ncol):
            wsend(d).start()
        wbuf[...] = av[0:sl, 0:n]

    with_identity(work, out1[0:n, :])
    chol_inv(work, rows, {j: functools.partial(early.forward, j) for j in range(4)})
    l1, l1i = factors(rows)

    xr = mm(p_ref[...], l1i, NT)
    src2[...] = mm(xr, xr, TN)
    red = Reduce(out2, red2[1], red2[0], red2[2:], ncol, z_first=True)
    red.start_first(src2)
    l1_ref[...] = l1
    lead_ref[:, 0:n] = xr
    xt = mm(out1[n:, :], l1i, NT)

    @pl.when(c != 0)
    def _():
        wsend(1).wait_recv()

    yw[part(0), n:] = wbuf[...]
    share(slice(n, 2 * n), vs, vr_sem)
    red.start_second()

    def block(k):
        early.block(k)
        xk = mm(pc[k], l1i, NT)
        vc_ref[k] = xk
        return mm3(halves(av[:, k * height:(k + 1) * height]), halves(xk))

    acc = block(0)
    acc = acc + block(1)
    acc = acc + block(2)
    red.start_c()
    acc = acc + block(3)
    yp[...] = acc
    early.finish(3)
    ybuf[0] = yp[part(0), :]
    for d in range(1, ncol):
        send(yp.at[part(d), :], ybuf.at[d], ys, yr, gc[d])
    red.finish()

    def spread():
        all_in(ybuf.at[1:ncol], yr, gc[1])
        yw[part(0), 0:n] = slot_sum(ybuf, c, ncol)
        share(slice(0, n), fs, fr)

    with_identity(work, out2[...])
    chol_inv(work, rows, {1: spread})
    l2, l2i = factors(rows)
    all_in(rest(slice(n, 2 * n)), vr_sem, gc[1])
    all_in(rest(slice(0, n)), fr, gc[1])

    avr[...] = mm(yw[:, 0:n], l2i, NT) + yw[:, n:]
    late.start_one()
    vr = mm(lead_ref[:, 0:n], l2i, NT) + jnp.where(eyes((height, n), row * height), 1.0, 0.0)
    src3[...] = mm(vr, avr[...], TN)
    red = Reduce(out3, red3[0], red3[1], red3[2:], ncol)
    red.start_first(src3)
    with_identity(work, mm(xt, l2i, NT).T + jnp.where(eyes((n, n)), 1.0, 0.0))
    near = (1, 3)
    gj_inverse(work, {4: red.start_second, 6: lambda: late.forward(0, near)})
    k = work[:, n:]

    def vectors(j):
        shift = (c * 4 + j) * height
        vc_ref[j] = mm(vc_ref[j], l2i, NT) + jnp.where(eyes((height, n), shift), 1.0, 0.0)

    late.forward(1, near)
    red.start_c()
    late.forward(2, near)
    late.forward(3, near)
    vectors(0)
    late.relay(0)
    vectors(1)
    late.relay(1)
    vectors(2)
    late.relay(2)
    vectors(3)
    band_ref[...] = -mm(l2, l1_ref[...], (((0,), (1,)), ((), ())))
    late.relay(3)
    red.finish()
    inner = mm(k, mm(out3[...], k), TN)
    right = jnp.concatenate([
        jnp.concatenate([jnp.zeros((n, n), F32), k], axis=1),
        jnp.concatenate([k.T, -0.5 * (inner + inner.T)], axis=1)], axis=0)
    lead_ref[...] = mm(jnp.concatenate([avr[...], vr], axis=1), right)
    for j in range(4):
        late.relayed(late.nearest(j))
    late.finish(2)
    all_out(ybuf.at[1:ncol], ys, gc[1])
    all_out(rest(slice(0, n)), fs, gc[1])
    all_out(rest(slice(n, 2 * n)), vs, gc[1])

    @pl.when(c == 0)
    def _():
        all_out(rest(slice(0, n)), ws, gc[1])


def last_kernel(l1_in, band_in, lead_ref, avc_ref, vc_ref, a_ref, out_ref, band_ref, l1_ref, obuf, outsem):
    width = avc_ref.shape[1]
    lead = halves(lead_ref[...])
    stores = []
    for k in range(4):
        cols = slice(k * width, (k + 1) * width)
        tail = halves(jnp.concatenate([avc_ref[k], vc_ref[k]], axis=1))
        obuf[k] = a_ref[:, cols] - mm3(lead, tail, NT)
        copy = pltpu.make_async_copy(obuf.at[k], out_ref.at[:, cols], outsem.at[k])
        copy.start()
        stores.append(copy)
    band_ref[...] = band_in[...]
    l1_ref[...] = l1_in[...]
    for copy in stores:
        copy.wait()


def body(ncol, panel, trailing):
    n = panel.shape[1]
    height, width = trailing.shape
    sl = height // ncol
    dma = pltpu.SemaphoreType.DMA

    def vmem(*shape):
        return pltpu.VMEM(shape, F32)

    l1, band, lead, avc, vc, kept = pl.pallas_call(
        functools.partial(main_kernel, ncol),
        out_shape=(vmem(n, n), vmem(n, n), vmem(height, 2 * n), vmem(4, height, n), vmem(4, height, n), vmem(height, width)),
        in_specs=[ANY, ANY], out_specs=(VM,) * 6,
        scratch_shapes=[vmem(2 * n, n), vmem(2 * n, n), vmem(n, n), vmem(n, n), vmem(n, n), vmem(n, n)]
        + reduce_scratch(2 * n, ncol) + reduce_scratch(n, ncol) + reduce_scratch(n, ncol)
        + gather_sems() + gather_sems()
        + [vmem(4, height, n), vmem(n, 2 * n), vmem(n, 2 * n), vmem(height, n),
           vmem(ncol, sl, n), vmem(sl, n), vmem(height, 2 * n), vmem(height, n),
           vmem(height, n)]
        + [dma, dma, dma, dma, dma, dma, dma, dma, dma, dma],
        compiler_params=pltpu.CompilerParams(collective_id=0, has_side_effects=True, vmem_limit_bytes=56 << 20),
        name="main")(panel, trailing)
    reduced, band, l1 = pl.pallas_call(
        last_kernel, out_shape=(struct(height, width), struct(n, n), struct(n, n)),
        in_specs=[VM] * 6, out_specs=(ANY, VM, VM),
        scratch_shapes=[vmem(4, height, width // 4), dma((4,))],
        compiler_params=pltpu.CompilerParams(vmem_limit_bytes=32 << 20), name="last",
    )(l1, band, lead, avc, vc, kept)
    return reduced, band, l1


def solution(mesh):
    return jax.shard_map(
        functools.partial(body, mesh.shape["col"]), mesh=mesh, in_specs=(P("row", None), P("row", "col")),
        out_specs=(P("row", "col"), P(), P()), check_vma=False)
```
